512 devices in a mesh: bond: 32 (over z_lo, x, core), leg: 16 (over z_hi, y).
Axes of the slice: x: 4, y: 4, z: 16 (z_hi: 4, z_lo: 4; z = z_hi * 4 + z_lo), core: 2. Of those that a mesh axis runs over, the one named last changes fastest.
Arguments:
- amplitudes: float32 [2, 1024, 262144], P(None, 'bond', 'leg'), may hold values from -6 to 6
- vectors: float32 [64, 262144], P(None, ('leg', 'bond')), may hold values from -0.01171875 to 0.01171875
- row_map: float32 [64, 4096], P('leg'), may hold values from -0.09375 to 0.09375
- col_map: float32 [64, 4096], P('bond'), may hold values from -0.09375 to 0.09375
Outputs:
- coarse: float32 [2, 8, 64, 64], P(None, None, 'leg', 'bond')
The draws below stay inside these ranges and needn't reach their ends.
All inputs are finite; a program needn't handle non-finite values.
Results may differ from the reference program's by a relative error of at most 0.00014.
Values sent between devices are 32-bit elements; how exact they have to be, the bound alone decides.
A program may use at most 64 MiB of HBM per device.

```python
import jax
import jax.numpy as jnp
from jax import lax

D = 64
K = 262144
ZS = 16


def block_levels(rng, dims, split, least, largest):
    def one(position, parts):
        steps = jax.random.uniform(jax.random.fold_in(jax.random.fold_in(rng, 6), position), (parts,), jnp.float32, least / len(split), largest / len(split))
        return jnp.repeat(jnp.exp(steps), dims[position] // parts).reshape((-1,) + (1,) * (len(dims) - position - 1))

    gain = one(*split[0])
    for cut in split[1:]:
        gain = gain * one(*cut)
    return gain


def centred(own_key, shape, deviation, limit, shards=(), held_as=jnp.bfloat16):
    level = block_levels(own_key, shape, shards, -0.22, 0.18) if shards else 1.0
    drawn = jax.random.normal(own_key, shape, jnp.float32) * deviation * level
    return jnp.minimum(jnp.maximum(drawn, -limit), limit).astype(held_as)


def setup_inputs(seed: int = 0) -> dict:
    keys = jax.random.split(jax.random.key(seed), 5)
    amplitudes = centred(keys[0], (2, ZS * D, K), 1.0, 6.0, ((1, 32), (2, 16)), jnp.float32)
    vectors = centred(keys[1], (D, K), K ** -0.5, 0.01171875, ((1, 512),), jnp.float32)
    row_map = centred(keys[2], (D, D * D), (D * D) ** -0.5, 0.09375, ((0, 16),), jnp.float32)
    col_map = centred(keys[3], (D, D * D), (D * D) ** -0.5, 0.09375, ((0, 32),), jnp.float32)
    return {"amplitudes": amplitudes, "vectors": vectors, "row_map": row_map, "col_map": col_map}


def coarsen(slab, row_maps, col_maps):
    highest = lax.Precision.HIGHEST
    even = slab[:, 0::2]
    odd = slab[:, 1::2]
    inner = jnp.einsum('ztjc,qcd->ztqjd', even, col_maps, precision=highest)
    real_part = jnp.einsum('tqjd,tkd->tqjk', inner[0], odd[0], precision=highest) - jnp.einsum('tqjd,tkd->tqjk', inner[1], odd[1], precision=highest)
    imag_part = jnp.einsum('tqjd,tkd->tqjk', inner[0], odd[1], precision=highest) + jnp.einsum('tqjd,tkd->tqjk', inner[1], odd[0], precision=highest)
    paired = jnp.stack([real_part, imag_part])
    return jnp.einsum('pjk,ztqjk->ztpq', row_maps, paired, precision=highest)


def reference(amplitudes, vectors, row_map, col_map):
    projected = jnp.einsum('jk,zrk->zjr', vectors, amplitudes, precision=lax.Precision.HIGHEST)
    slab = projected.reshape(2, D, ZS, D).transpose(0, 2, 1, 3)
    return coarsen(slab, row_map.reshape(D, D, D), col_map.reshape(D, D, D))
```

```python
import functools

import jax
import jax.numpy as jnp
from jax import lax
from jax.experimental import pallas as pl
from jax.experimental.pallas import tpu as pltpu
from jax.sharding import PartitionSpec as P

MESH = pl.DeviceIdType.MESH
F32, BF16 = jnp.float32, jnp.bfloat16
NT = (((1,), (1,)), ((), ()))
NN = (((1,), (0,)), ((), ()))


def halves(v):
    hi = v.astype(BF16)
    return hi, (v - hi.astype(F32)).astype(BF16)


def kernel(
    amp, vec, rmap, cmap, out,
    abuf, vbuf, rbuf, cbuf, acc, part, piece8, piece4, slabs, rwide, rcat, ccat, bcat, gbuf, hbuf, msg, res,
    a_in, a_rin, a_rout, v_in, z_in, x_in, v_out, map_in, c_in, c_out,
    p8_in, p8_out, p4_in, p4_out, s_in, s_out, m_in, m_out,
):
    bond, leg = lax.axis_index("bond"), lax.axis_index("leg")
    core, x, zl = lax.rem(bond, 2), lax.rem(bond // 2, 4), bond // 8
    y, zh = lax.rem(leg, 4), leg // 4

    def dev(x_=x, zl_=zl, core_=core, y_=y, zh_=zh):
        return ((zl_ * 4 + x_) * 2 + core_, zh_ * 4 + y_)

    def rot(v, d):
        return lax.rem(v + (d + 4), 4)

    def remote(src, dst, send, recv, device):
        return pltpu.make_async_remote_copy(
            src_ref=src, dst_ref=dst, send_sem=send, recv_sem=recv, device_id=device, device_id_type=MESH
        )

    def drain(ref, sem):
        pltpu.make_async_copy(ref, ref, sem).wait()

    barrier = pltpu.get_barrier_semaphore()

    def greet(device):
        pl.semaphore_signal(barrier, inc=1, device_id=device, device_id_type=MESH)

    def row_peer(k):
        flat = lax.rem(((x * 4 + y) * 2 + core) + k, 32)
        return flat // 8, lax.rem(flat // 2, 4), lax.rem(flat, 2)

    @pl.loop(1, 32)
    def _(k):
        x_, y_, core_ = row_peer(k)
        greet(dev(x_=x_, y_=y_, core_=core_))

    for d in (1, 2, 3):
        greet(dev(zl_=rot(zl, d)))
        greet(dev(zh_=rot(zh, d)))

    own = zl * 4 + x
    pltpu.make_async_copy(vec, vbuf.at[own], v_in).start()
    map_copies = (pltpu.make_async_copy(rmap, rbuf, map_in.at[0]), pltpu.make_async_copy(cmap, cbuf.at[zl], map_in.at[1]))
    for copy in map_copies:
        copy.start()

    def block_of(i, xo):
        return rot(zl, -i) * 4 + rot(x, xo)

    def a_local(n):
        cols = pl.ds(pl.multiple_of((n * 2 + core) * 512, 512), 512)
        return pltpu.make_async_copy(amp.at[:, cols], abuf.at[core, n], a_in.at[n])

    def a_remote(n):
        cols = pl.ds(pl.multiple_of((n * 2 + 1 - core) * 512, 512), 512)
        return remote(amp.at[:, cols], abuf.at[core, n], a_rout, a_rin.at[n], dev(core_=1 - core))

    pl.semaphore_wait(barrier, 37)

    def x_send(i, k):
        half, way = ((0, 1), (1, -1), (1, 1), (0, -1))[k]
        n, rows = block_of(i, 0), pl.ds(half * 32, 32)
        src = vbuf.at[n, rows]
        return remote(src, vbuf.at[n, rows], v_out, x_in.at[i, k], dev(x_=rot(x, way)))

    def x_relay(i, k):
        half, way = ((0, 1), (1, -1))[k]
        n, rows = block_of(i, -way), pl.ds(half * 32, 32)
        return remote(vbuf.at[n, rows], vbuf.at[n, rows], v_out, x_in.at[i, 4 + k], dev(x_=rot(x, way)))

    z_sends = [
        remote(vec, vbuf.at[own], v_out, z_in.at[d - 1], dev(zl_=rot(zl, d))) for d in (1, 2, 3)
    ]
    for half, way, k in ((0, 1, 0), (1, -1, 1)):
        rows = pl.ds(half * 32, 32)
        remote(vec.at[rows], vbuf.at[own, rows], v_out, x_in.at[0, k], dev(x_=rot(x, way))).start()
    z_sends[0].start()
    for half, way, k in ((1, 1, 2), (0, -1, 3)):
        rows = pl.ds(half * 32, 32)
        remote(vec.at[rows], vbuf.at[own, rows], v_out, x_in.at[0, k], dev(x_=rot(x, way))).start()
    z_sends[1].start()
    z_sends[2].start()

    @pl.loop(0, 16)
    def _(m):
        n = block_of(m // 4, lax.rem(m, 4))
        a_local(n).start()
        a_remote(n).start()

    acc[...] = jnp.zeros_like(acc)

    def project(n):
        a_local(n).wait()
        a_remote(n).wait_recv()
        a_hi, a_lo = halves(abuf[:, n].reshape(128, 512))
        v_hi, v_lo = halves(vbuf[n])
        acc[...] += lax.dot_general(
            jnp.concatenate([a_hi, a_lo], 0), jnp.concatenate([v_hi, v_lo], 0), NT, preferred_element_type=F32
        )

    def relay(i):
        for k in (0, 1):
            x_send(i, k).wait_recv()
            x_relay(i, k).start()

    def far(i):
        for k in (0, 1):
            x_relay(i, k).wait_recv()
        project(block_of(i, 2))

    for copy in map_copies:
        copy.wait()
    c_sends = [
        remote(cbuf.at[zl], cbuf.at[zl], c_out, c_in.at[d - 1], dev(zl_=rot(zl, d))) for d in (1, 2, 3)
    ]
    for copy in c_sends:
        copy.start()
    relay(0)

    def maps():
        first = lax.broadcasted_iota(jnp.int32, (32, 128), 1) < 64
        for p in range(4):
            v = rbuf[:, p, :]
            swapped = pltpu.roll(v, 64, 1)
            for par in range(2):
                low, high = (v, swapped) if par == 0 else (swapped, v)
                rwide[p, pl.ds(par, 32, stride=2)] = jnp.where(first, low, 0.0)
                rwide[p, pl.ds(64 + par, 32, stride=2)] = jnp.where(first, 0.0, high)
            hi, lo = halves(rwide[p])
            for k, w in enumerate((hi, hi, lo)):
                rcat[k * 128 : k * 128 + 128, p * 128 : p * 128 + 128] = w
        bcat[...] = jnp.zeros_like(bcat)
        for d in (1, 2, 3):
            c_sends[d - 1].wait_recv()
        for k in range(4):
            for q in range(2):
                hi, lo = halves(cbuf[k, :, q, :])
                ccat[k * 64 + q * 32 : k * 64 + q * 32 + 32] = jnp.concatenate([hi, lo, hi], 1)

    @pl.loop(0, 4)
    def _(i):
        @pl.when(i < 3)
        def _():
            remote(vec, vbuf.at[own], v_out, z_in.at[i], dev()).wait_recv()
            for k in range(4):
                x_send(i + 1, k).start()

        @pl.when(i > 0)
        def _():
            relay(i)

        @pl.when(i == 0)
        def _():
            pltpu.make_async_copy(vec, vbuf.at[own], v_in).wait()

        project(block_of(i, 0))

        @pl.when(i > 0)
        def _():
            far(i - 1)

        x_send(i, 2).wait_recv()
        project(block_of(i, -1))
        x_send(i, 3).wait_recv()
        project(block_of(i, 1))

        @pl.when(i == 0)
        def _():
            maps()

    far(3)

    both = acc[:128] + acc[128:]
    both = both + pltpu.roll(both, 64, 1)
    first = lax.broadcasted_iota(jnp.int32, (32, 128), 1) < 64
    for s in range(2):
        part[s * 32 : s * 32 + 32] = jnp.where(first, both[s * 64 : s * 64 + 32], both[s * 64 + 32 : s * 64 + 64])

    mine = y * 2 + core

    def eighth(k):
        return pl.ds(pl.multiple_of(k * 8, 8), 8)

    def scatter(k):
        to = lax.rem(mine + k, 8)
        return remote(part.at[eighth(to)], piece8.at[mine], p8_out, p8_in.at[k - 1], dev(y_=to // 2, core_=lax.rem(to, 2)))

    for k in range(1, 8):
        scatter(k).start()
    piece8[mine] = part[eighth(mine)]
    for k in range(1, 8):
        scatter(k).wait_recv()
    piece4[zh] = jnp.sum(piece8[...], axis=0)

    def spread(d):
        return remote(piece4.at[zh], piece4.at[zh], p4_out, p4_in.at[d - 1], dev(zh_=rot(zh, d)))

    for d in (2, 1, 3):
        spread(d).start()
    for d in (1, 2, 3):
        spread(d).wait_recv()
    here = pl.ds(pl.multiple_of(x * 64 + mine * 8, 8), 8)
    slabs[here] = jnp.sum(piece4[...], axis=0)

    @pl.loop(1, 32)
    def _(k):
        x_, y_, core_ = row_peer(k)
        remote(slabs.at[here], slabs.at[here], s_out, s_in, dev(x_=x_, y_=y_, core_=core_)).start()

    drain(slabs.at[pl.ds(0, 248)], s_in)

    lhs = jnp.concatenate(
        [slabs[pl.ds(t * 128 + par, 32, stride=2)] for t in range(2) for par in range(2)], 0
    )
    l_hi, l_lo = halves(lhs)
    gbuf[...] = lax.dot_general(
        jnp.concatenate([l_hi, l_lo, l_hi], 1), rcat[...], NN, preferred_element_type=F32
    )
    for t in range(2):
        b_hi, b_lo = halves(slabs[t * 128 + 64 : t * 128 + 128])
        for k, v in enumerate((b_hi, b_hi, b_lo)):
            for par in range(2):
                bcat[t, k * 128 + par * 64 : k * 128 + par * 64 + 64, par * 128 : par * 128 + 128] = v
        hbuf[t] = lax.dot_general(ccat[...], bcat[t], NN, preferred_element_type=F32)

    @pl.loop(0, 4)
    def _(to):
        for t in range(2):
            sums = [[None] * 2 for _ in range(8)]
            for q in range(2):
                rows = pl.ds(pl.multiple_of(to * 64 + q * 32, 32), 32)
                h = [hbuf[t, rows, par * 128 : par * 128 + 128] for par in range(2)]
                for p in range(4):
                    g = [gbuf[t * 64 + par * 32 : t * 64 + par * 32 + 32, p * 128 : p * 128 + 128] for par in range(2)]
                    straight = g[0] * h[0] + g[1] * h[1]
                    crossed = pltpu.roll(g[0], 64, 1) * h[0] + pltpu.roll(g[1], 64, 1) * h[1]
                    sums[p][q] = jnp.sum(straight, axis=0, keepdims=True)
                    sums[4 + p][q] = jnp.sum(crossed, axis=0, keepdims=True)
            msg[to, t] = jnp.concatenate([v for pair in sums for v in pair], 0)

    def answer(d):
        return remote(msg.at[rot(zl, d)], res.at[zl], m_out, m_in.at[d - 1], dev(zl_=rot(zl, d)))

    for d in (1, 2, 3):
        answer(d).start()
    res[zl] = msg[zl]
    for d in (1, 2, 3):
        answer(d).wait_recv()
    row = lax.broadcasted_iota(jnp.int32, (16, 128), 0)
    lane = lax.broadcasted_iota(jnp.int32, (16, 128), 1)
    minus = jnp.logical_and(row < 8, lane >= 64)
    total = jnp.zeros((16, 128), F32)
    for k in range(8):
        v = res[k // 2, k % 2]
        total = total + jnp.where(lane == k, jnp.sum(jnp.where(minus, -v, v), axis=1, keepdims=True), 0.0)
    out[...] = total[:, :8]

    drain(vbuf.at[pl.ds(0, 15)], v_out)
    drain(abuf.at[0], a_rout)
    drain(cbuf.at[pl.ds(0, 3)], c_out)
    drain(piece8.at[pl.ds(0, 7)], p8_out)
    drain(piece4.at[pl.ds(0, 3)], p4_out)
    drain(slabs.at[pl.ds(0, 248)], s_out)
    drain(res.at[pl.ds(0, 3)], m_out)


def local(amplitudes, vectors, row_map, col_map):
    dma = pltpu.SemaphoreType.DMA
    got = pl.pallas_call(
        kernel,
        out_shape=jax.ShapeDtypeStruct((16, 8), F32),
        in_specs=[pl.BlockSpec(memory_space=pl.ANY)] * 4,
        out_specs=pl.BlockSpec(memory_space=pltpu.VMEM),
        scratch_shapes=[
            pltpu.VMEM((2, 16, 64, 512), F32),
            pltpu.VMEM((16, 64, 512), F32),
            pltpu.VMEM((32, 4, 128), F32),
            pltpu.VMEM((4, 32, 2, 128), F32),
            pltpu.VMEM((256, 128), F32),
            pltpu.VMEM((64, 128), F32),
            pltpu.VMEM((8, 8, 128), F32),
            pltpu.VMEM((4, 8, 128), F32),
            pltpu.VMEM((256, 128), F32),
            pltpu.VMEM((4, 128, 128), F32),
            pltpu.VMEM((384, 512), BF16),
            pltpu.VMEM((256, 384), BF16),
            pltpu.VMEM((2, 384, 256), BF16),
            pltpu.VMEM((128, 512), F32),
            pltpu.VMEM((2, 256, 256), F32),
            pltpu.VMEM((4, 2, 16, 128), F32),
            pltpu.VMEM((4, 2, 16, 128), F32),
            dma((16,)), dma((16,)), dma, dma, dma((3,)), dma((4, 6)), dma, dma((2,)), dma((3,)), dma,
            dma((7,)), dma, dma((3,)), dma, dma, dma, dma((3,)), dma,
        ],
        compiler_params=pltpu.CompilerParams(collective_id=0, has_side_effects=True),
    )(
        amplitudes.reshape(64, -1),
        vectors,
        row_map.reshape(4, 32, 128).transpose(1, 0, 2),
        col_map.reshape(2, 32, 128).transpose(1, 0, 2),
    )
    return got.reshape(2, 4, 2, 8).transpose(0, 3, 1, 2)


def solution(mesh):
    return jax.shard_map(
        local,
        mesh=mesh,
        in_specs=(
            P(None, "bond", "leg"),
            P(None, ("leg", "bond")),
            P("leg", None),
            P("bond", None),
        ),
        out_specs=P(None, None, "leg", "bond"),
        check_vma=False,
    )
```

```python
import functools

import jax
import jax.numpy as jnp
from jax import lax
from jax.experimental import pallas as pl
from jax.experimental.pallas import tpu as pltpu
from jax.sharding import PartitionSpec as P

MESH = pl.DeviceIdType.MESH
F32, BF16 = jnp.float32, jnp.bfloat16
NT = (((1,), (1,)), ((), ()))
NN = (((1,), (0,)), ((), ()))


def halves(v):
    hi = v.astype(BF16)
    return hi, (v - hi.astype(F32)).astype(BF16)


def kernel(
    amp, vec, rmap, cmap, out,
    abuf, vbuf, rbuf, cbuf, acc, part, piece8, piece4, slabs, rwide, rcat, ccat, bcat, gbuf, hbuf, msg, res,
    a_in, a_rin, a_rout, v_in, z_in, x_in, v_out, map_in, c_in, c_out,
    p8_in, p8_out, p4_in, p4_out, s_in, s_out, m_in, m_out, word,
):
    bond, leg = lax.axis_index("bond"), lax.axis_index("leg")
    core, x, zl = lax.rem(bond, 2), lax.rem(bond // 2, 4), bond // 8
    y, zh = lax.rem(leg, 4), leg // 4

    def dev(x_=x, zl_=zl, core_=core, y_=y, zh_=zh):
        return ((zl_ * 4 + x_) * 2 + core_, zh_ * 4 + y_)

    def rot(v, d):
        return lax.rem(v + (d + 4), 4)

    def remote(src, dst, send, recv, device):
        return pltpu.make_async_remote_copy(
            src_ref=src, dst_ref=dst, send_sem=send, recv_sem=recv, device_id=device, device_id_type=MESH
        )

    def drain(ref, sem):
        pltpu.make_async_copy(ref, ref, sem).wait()

    def up(d):
        z_ = lax.rem(zh * 4 + zl + (d + 16), 16)
        return dev(zl_=lax.rem(z_, 4), zh_=z_ // 4)

    beside = [dev(x_=rot(x, d)) for d in (1, -1)] + [dev(y_=rot(y, d)) for d in (1, -1)] + [up(1), up(-1)]
    partner = dev(core_=1 - core)
    rounds = (beside, [partner, up(2), up(-2)], [dev(y_=rot(y, d)) for d in (1, 2, 3)] + [up(4), up(-4)])

    def tell(sem, devices):
        for device in devices:
            pl.semaphore_signal(sem, inc=1, device_id=device, device_id_type=MESH)

    barrier = pltpu.get_barrier_semaphore()
    tell(barrier, beside + [partner])

    own = zl * 4 + x
    pltpu.make_async_copy(vec, vbuf.at[own], v_in).start()
    map_copies = (pltpu.make_async_copy(rmap, rbuf, map_in.at[0]), pltpu.make_async_copy(cmap, cbuf.at[zl], map_in.at[1]))
    for copy in map_copies:
        copy.start()

    def row_of(i):
        low, odd = zl < 2, lax.rem(zl, 2) == 1
        first = jnp.where(odd, 2, 1)
        second = jnp.where(odd, jnp.where(low, 0, 1), jnp.where(low, 2, 3))
        third = jnp.where(low, 3, 0)
        return jnp.where(i == 0, zl, jnp.where(i == 1, first, jnp.where(i == 2, second, third)))

    def block_of(i, xo):
        return row_of(i) * 4 + rot(x, xo)

    def a_local(n):
        cols = pl.ds(pl.multiple_of((n * 2 + core) * 512, 512), 512)
        return pltpu.make_async_copy(amp.at[:, cols], abuf.at[core, n], a_in.at[n])

    def a_remote(n):
        cols = pl.ds(pl.multiple_of((n * 2 + 1 - core) * 512, 512), 512)
        return remote(amp.at[:, cols], abuf.at[core, n], a_rout, a_rin.at[n], dev(core_=1 - core))

    pl.semaphore_wait(barrier, 7)
    tell(word.at[0], rounds[0])

    def x_send(i, k):
        half, way = ((0, 1), (1, -1), (1, 1), (0, -1))[k]
        n, rows = block_of(i, 0), pl.ds(half * 32, 32)
        src = vbuf.at[n, rows]
        return remote(src, vbuf.at[n, rows], v_out, x_in.at[i, k], dev(x_=rot(x, way)))

    def x_relay(i, k):
        half, way = ((0, 1), (1, -1))[k]
        n, rows = block_of(i, -way), pl.ds(half * 32, 32)
        return remote(vbuf.at[n, rows], vbuf.at[n, rows], v_out, x_in.at[i, 4 + k], dev(x_=rot(x, way)))

    middle = jnp.logical_and(zl > 0, zl < 3)

    def z_send(i):
        return remote(vec, vbuf.at[own], v_out, z_in.at[zl], dev(zl_=row_of(i)))

    def z_take(i):
        r = row_of(i)
        n = r * 4 + x
        remote(vec, vbuf.at[n], v_out, z_in.at[r], dev()).wait_recv()

        @pl.when(middle)
        def _():
            to = jnp.where(r > zl, zl - 1, zl + 1)
            remote(vbuf.at[n], vbuf.at[n], v_out, z_in.at[r], dev(zl_=to)).start()

    for half, way, k in ((0, 1, 0), (1, -1, 1), (1, 1, 2), (0, -1, 3)):
        rows = pl.ds(half * 32, 32)
        remote(vec.at[rows], vbuf.at[own, rows], v_out, x_in.at[0, k], dev(x_=rot(x, way))).start()
        if k == 1:
            z_send(1).start()

            @pl.when(middle)
            def _():
                z_send(2).start()
    for m in range(4):
        a_local(block_of(0, m)).start()
        a_remote(block_of(0, m)).start()
    pl.semaphore_wait(word.at[0], 6)
    tell(word.at[1], rounds[1])
    @pl.loop(4, 16)
    def _(m):
        n = block_of(m // 4, lax.rem(m, 4))
        a_local(n).start()
        a_remote(n).start()

    pl.semaphore_wait(word.at[1], 3)
    tell(word.at[2], rounds[2])

    acc[...] = jnp.zeros_like(acc)

    def project(n):
        a_local(n).wait()
        a_remote(n).wait_recv()
        a_hi, a_lo = halves(abuf[:, n].reshape(128, 512))
        v_hi, v_lo = halves(vbuf[n])
        acc[...] += lax.dot_general(
            jnp.concatenate([a_hi, a_lo], 0), jnp.concatenate([v_hi, v_lo], 0), NT, preferred_element_type=F32
        )

    def relay(i):
        for k in (0, 1):
            x_send(i, k).wait_recv()
            x_relay(i, k).start()

    def far(i):
        for k in (0, 1):
            x_relay(i, k).wait_recv()
        project(block_of(i, 2))

    relay(0)
    for copy in map_copies:
        copy.wait()
    c_sends = [
        remote(cbuf.at[zl], cbuf.at[zl], c_out, c_in.at[d - 1], dev(zl_=rot(zl, d))) for d in (1, 2, 3)
    ]

    def maps():
        first = lax.broadcasted_iota(jnp.int32, (32, 128), 1) < 64
        for p in range(4):
            v = rbuf[:, p, :]
            swapped = pltpu.roll(v, 64, 1)
            for par in range(2):
                low, high = (v, swapped) if par == 0 else (swapped, v)
                rwide[p, pl.ds(par, 32, stride=2)] = jnp.where(first, low, 0.0)
                rwide[p, pl.ds(64 + par, 32, stride=2)] = jnp.where(first, 0.0, high)
            hi, lo = halves(rwide[p])
            for k, w in enumerate((hi, hi, lo)):
                rcat[k * 128 : k * 128 + 128, p * 128 : p * 128 + 128] = w
        bcat[...] = jnp.zeros_like(bcat)
        for d in (1, 2, 3):
            c_sends[d - 1].wait_recv()
        for k in range(4):
            for q in range(2):
                hi, lo = halves(cbuf[k, :, q, :])
                ccat[k * 64 + q * 32 : k * 64 + q * 32 + 32] = jnp.concatenate([hi, lo, hi], 1)

    @pl.loop(0, 4)
    def _(i):
        @pl.when(i < 3)
        def _():
            @pl.when(jnp.logical_or(i == 0, jnp.logical_not(middle)))
            def _():
                z_take(i + 1)

            for k in range(4):
                x_send(i + 1, k).start()

        @pl.when(jnp.logical_and(i < 2, middle))
        def _():
            z_take(i + 2)

        @pl.when(i == 2)
        def _():
            for copy in c_sends:
                copy.start()

        @pl.when(i > 0)
        def _():
            relay(i)

        @pl.when(i == 0)
        def _():
            pltpu.make_async_copy(vec, vbuf.at[own], v_in).wait()

        project(block_of(i, 0))

        @pl.when(i > 0)
        def _():
            far(i - 1)

        x_send(i, 2).wait_recv()
        project(block_of(i, -1))
        x_send(i, 3).wait_recv()
        project(block_of(i, 1))

    far(3)

    both = acc[:128] + acc[128:]
    both = both + pltpu.roll(both, 64, 1)
    first = lax.broadcasted_iota(jnp.int32, (32, 128), 1) < 64
    for s in range(2):
        part[s * 32 : s * 32 + 32] = jnp.where(first, both[s * 64 : s * 64 + 32], both[s * 64 + 32 : s * 64 + 64])

    pl.semaphore_wait(word.at[2], 5)
    mine = y * 2 + core

    def eighth(k):
        return pl.ds(pl.multiple_of(k * 8, 8), 8)

    def scatter(k):
        to = lax.rem(mine + k, 8)
        return remote(part.at[eighth(to)], piece8.at[mine], p8_out, p8_in.at[k - 1], dev(y_=to // 2, core_=lax.rem(to, 2)))

    for k in (5, 4, 3, 2, 6, 7, 1):
        scatter(k).start()
    piece8[mine] = part[eighth(mine)]
    for k in range(1, 8):
        scatter(k).wait_recv()
    piece4[zh] = jnp.sum(piece8[...], axis=0)

    def spread(d):
        return remote(piece4.at[zh], piece4.at[zh], p4_out, p4_in.at[d - 1], dev(zh_=rot(zh, d)))

    for d in (2, 1, 3):
        spread(d).start()
    maps()
    for d in (1, 2, 3):
        spread(d).wait_recv()
    here = pl.ds(pl.multiple_of(x * 64 + mine * 8, 8), 8)
    slabs[here] = jnp.sum(piece4[...], axis=0)

    for dx in (2, 1, 3, 0):
        for dy in (2, 1, 3, 0):
            for core_ in (1 - core, core):
                if dx or dy or core_ is not core:
                    to = dev(x_=rot(x, dx), y_=rot(y, dy), core_=core_)
                    remote(slabs.at[here], slabs.at[here], s_out, s_in, to).start()

    drain(slabs.at[pl.ds(0, 248)], s_in)

    lhs = jnp.concatenate(
        [slabs[pl.ds(t * 128 + par, 32, stride=2)] for t in range(2) for par in range(2)], 0
    )
    l_hi, l_lo = halves(lhs)
    gbuf[...] = lax.dot_general(
        jnp.concatenate([l_hi, l_lo, l_hi], 1), rcat[...], NN, preferred_element_type=F32
    )
    for t in range(2):
        b_hi, b_lo = halves(slabs[t * 128 + 64 : t * 128 + 128])
        for k, v in enumerate((b_hi, b_hi, b_lo)):
            for par in range(2):
                bcat[t, k * 128 + par * 64 : k * 128 + par * 64 + 64, par * 128 : par * 128 + 128] = v
        hbuf[t] = lax.dot_general(ccat[...], bcat[t], NN, preferred_element_type=F32)

    row = lax.broadcasted_iota(jnp.int32, (16, 128), 0)
    lane = lax.broadcasted_iota(jnp.int32, (16, 128), 1)
    minus = jnp.logical_and(row < 8, lane >= 64)

    @pl.loop(0, 4)
    def _(to):
        total = jnp.zeros((16, 128), F32)
        for t in range(2):
            sums = [[None] * 2 for _ in range(8)]
            for q in range(2):
                rows = pl.ds(pl.multiple_of(to * 64 + q * 32, 32), 32)
                h = [hbuf[t, rows, par * 128 : par * 128 + 128] for par in range(2)]
                for p in range(4):
                    g = [gbuf[t * 64 + par * 32 : t * 64 + par * 32 + 32, p * 128 : p * 128 + 128] for par in range(2)]
                    straight = g[0] * h[0] + g[1] * h[1]
                    crossed = pltpu.roll(g[0], 64, 1) * h[0] + pltpu.roll(g[1], 64, 1) * h[1]
                    sums[p][q] = jnp.sum(straight, axis=0, keepdims=True)
                    sums[4 + p][q] = jnp.sum(crossed, axis=0, keepdims=True)
            v = jnp.concatenate([v for pair in sums for v in pair], 0)
            v = jnp.sum(jnp.where(minus, -v, v), axis=1, keepdims=True)
            total = total + jnp.where(lane == zl * 2 + t, v, 0.0)
        msg[to] = total

    def answer(d):
        return remote(msg.at[rot(zl, d)], res.at[zl], m_out, m_in.at[d - 1], dev(zl_=rot(zl, d)))

    for d in (1, 2, 3):
        answer(d).start()
    res[zl] = msg[zl]
    for d in (1, 2, 3):
        answer(d).wait_recv()
    out[...] = jnp.sum(res[...], axis=0)[:, :8]

    drain(vbuf.at[pl.ds(0, 13)], v_out)

    @pl.when(middle)
    def _():
        drain(vbuf.at[pl.ds(0, 4)], v_out)

    drain(abuf.at[0], a_rout)
    drain(cbuf.at[pl.ds(0, 3)], c_out)
    drain(piece8.at[pl.ds(0, 7)], p8_out)
    drain(piece4.at[pl.ds(0, 3)], p4_out)
    drain(slabs.at[pl.ds(0, 248)], s_out)
    drain(res.at[pl.ds(0, 3)], m_out)


def local(amplitudes, vectors, row_map, col_map):
    dma = pltpu.SemaphoreType.DMA
    got = pl.pallas_call(
        kernel,
        out_shape=jax.ShapeDtypeStruct((16, 8), F32),
        in_specs=[pl.BlockSpec(memory_space=pl.ANY)] * 4,
        out_specs=pl.BlockSpec(memory_space=pltpu.VMEM),
        scratch_shapes=[
            pltpu.VMEM((2, 16, 64, 512), F32),
            pltpu.VMEM((16, 64, 512), F32),
            pltpu.VMEM((32, 4, 128), F32),
            pltpu.VMEM((4, 32, 2, 128), F32),
            pltpu.VMEM((256, 128), F32),
            pltpu.VMEM((64, 128), F32),
            pltpu.VMEM((8, 8, 128), F32),
            pltpu.VMEM((4, 8, 128), F32),
            pltpu.VMEM((256, 128), F32),
            pltpu.VMEM((4, 128, 128), F32),
            pltpu.VMEM((384, 512), BF16),
            pltpu.VMEM((256, 384), BF16),
            pltpu.VMEM((2, 384, 256), BF16),
            pltpu.VMEM((128, 512), F32),
            pltpu.VMEM((2, 256, 256), F32),
            pltpu.VMEM((4, 16, 128), F32),
            pltpu.VMEM((4, 16, 128), F32),
            dma((16,)), dma((16,)), dma, dma, dma((4,)), dma((4, 6)), dma, dma((2,)), dma((3,)), dma,
            dma((7,)), dma, dma((3,)), dma, dma, dma, dma((3,)), dma, pltpu.SemaphoreType.REGULAR((3,)),
        ],
        compiler_params=pltpu.CompilerParams(collective_id=0, has_side_effects=True),
    )(
        amplitudes.reshape(64, -1),
        vectors,
        row_map.reshape(4, 32, 128).transpose(1, 0, 2),
        col_map.reshape(2, 32, 128).transpose(1, 0, 2),
    )
    return got.reshape(2, 4, 2, 8).transpose(0, 3, 1, 2)


def solution(mesh):
    return jax.shard_map(
        local,
        mesh=mesh,
        in_specs=(
            P(None, "bond", "leg"),
            P(None, ("leg", "bond")),
            P("leg", None),
            P("bond", None),
        ),
        out_specs=P(None, None, "leg", "bond"),
        check_vma=False,
    )
```

```python
import functools

import jax
import jax.numpy as jnp
from jax import lax
from jax.experimental import pallas as pl
from jax.experimental.pallas import tpu as pltpu
from jax.sharding import PartitionSpec as P

MESH = pl.DeviceIdType.MESH
F32, BF16 = jnp.float32, jnp.bfloat16
NT = (((1,), (1,)), ((), ()))
NN = (((1,), (0,)), ((), ()))


def halves(v):
    hi = v.astype(BF16)
    return hi, (v - hi.astype(F32)).astype(BF16)


def kernel(
    amp, vec, rmap, cmap, out,
    abuf, vbuf, rbuf, cbuf, acc, part, piece8, piece4, slabs, rwide, rcat, ccat, bcat, gbuf, gswap, hbuf, msg, res,
    a_in, a_rin, a_rout, v_in, z_in, b_in, r_in, x_in, v_out, map_in, c_in, c_out,
    p8_in, p8_out, p4_in, p4_out, s_in, s_out, m_in, m_out, word,
):
    bond, leg = lax.axis_index("bond"), lax.axis_index("leg")
    core, x, zl = lax.rem(bond, 2), lax.rem(bond // 2, 4), bond // 8
    y, zh = lax.rem(leg, 4), leg // 4

    def dev(x_=x, zl_=zl, core_=core, y_=y, zh_=zh):
        return ((zl_ * 4 + x_) * 2 + core_, zh_ * 4 + y_)

    def rot(v, d):
        return lax.rem(v + (d + 4), 4)

    def remote(src, dst, send, recv, device):
        return pltpu.make_async_remote_copy(
            src_ref=src, dst_ref=dst, send_sem=send, recv_sem=recv, device_id=device, device_id_type=MESH
        )

    def drain(ref, sem):
        pltpu.make_async_copy(ref, ref, sem).wait()

    def up(d):
        z_ = lax.rem(zh * 4 + zl + (d + 16), 16)
        return dev(zl_=lax.rem(z_, 4), zh_=z_ // 4)

    beside = [dev(x_=rot(x, d)) for d in (1, -1)] + [dev(y_=rot(y, d)) for d in (1, -1)] + [up(1), up(-1)]
    partner = dev(core_=1 - core)
    rounds = (beside, [partner, up(2), up(-2)], [dev(y_=rot(y, d)) for d in (1, 2, 3)] + [up(4), up(-4)])

    def tell(sem, devices):
        for device in devices:
            pl.semaphore_signal(sem, inc=1, device_id=device, device_id_type=MESH)

    barrier = pltpu.get_barrier_semaphore()
    tell(barrier, beside + [partner])

    own = zl * 4 + x
    pltpu.make_async_copy(vec, vbuf.at[own], v_in).start()
    map_copies = (pltpu.make_async_copy(rmap, rbuf, map_in.at[0]), pltpu.make_async_copy(cmap, cbuf.at[zl], map_in.at[1]))
    for copy in map_copies:
        copy.start()

    def row_of(i):
        low, odd = zl < 2, lax.rem(zl, 2) == 1
        first = jnp.where(odd, 2, 1)
        second = jnp.where(odd, jnp.where(low, 0, 1), jnp.where(low, 2, 3))
        third = jnp.where(low, 3, 0)
        return jnp.where(i == 0, zl, jnp.where(i == 1, first, jnp.where(i == 2, second, third)))

    def block_of(i, xo):
        return row_of(i) * 4 + rot(x, xo)

    def a_local(n):
        cols = pl.ds(pl.multiple_of((n * 2 + core) * 512, 512), 512)
        return pltpu.make_async_copy(amp.at[:, cols], abuf.at[core, n], a_in.at[n])

    def a_remote(n):
        cols = pl.ds(pl.multiple_of((n * 2 + 1 - core) * 512, 512), 512)
        return remote(amp.at[:, cols], abuf.at[core, n], a_rout, a_rin.at[n], dev(core_=1 - core))

    pl.semaphore_wait(barrier, 7)
    tell(word.at[0], rounds[0])

    rest = pl.ds(56, 8)

    def rows(half):
        return (pl.ds(0, 32), pl.ds(32, 24))[half]

    def side(k):
        return pl.ds(k * 256, 256)

    kinds = ((0, 1), (1, -1), (1, 1), (0, -1))

    def x_send(i, half, k):
        ref = vbuf.at[block_of(i, 0), rows(half), side(kinds[k][0])]
        return remote(ref, ref, v_out, x_in.at[i, half, k], dev(x_=rot(x, kinds[k][1])))

    def x_relay(i, half, k):
        ref = vbuf.at[block_of(i, -kinds[k][1]), rows(half), side(kinds[k][0])]
        return remote(ref, ref, v_out, x_in.at[i, half, 4 + k], dev(x_=rot(x, kinds[k][1])))

    def r_send(k):
        return remote(vec.at[rest], vbuf.at[own, rest], v_out, r_in.at[k], dev(x_=rot(x, kinds[k][1])))

    def r_relay(k):
        ref = vbuf.at[zl * 4 + rot(x, -kinds[k][1]), rest, side(k)]
        return remote(ref, ref, v_out, r_in.at[2 + k], dev(x_=rot(x, kinds[k][1])))

    middle = jnp.logical_and(zl > 0, zl < 3)

    def b_copy(r, to):
        ref = vbuf.at[pl.ds(r * 4, 4), rest]
        return remote(ref, ref, v_out, b_in.at[r], dev(zl_=to))

    def b_take(i):
        r = row_of(i)
        copy = b_copy(r, jnp.where(r > zl, zl - 1, zl + 1))
        copy.wait_recv()

        @pl.when(middle)
        def _():
            copy.start()


    def z_send(i, half):
        return remote(vec.at[rows(half)], vbuf.at[own, rows(half)], v_out, z_in.at[zl, half], dev(zl_=row_of(i)))

    def z_take(i, half):
        r = row_of(i)
        ref = vbuf.at[r * 4 + x, rows(half)]
        copy = remote(ref, ref, v_out, z_in.at[r, half], dev(zl_=jnp.where(r > zl, zl - 1, zl + 1)))
        copy.wait_recv()

        @pl.when(middle)
        def _():
            copy.start()

        for k in range(4):
            x_send(i, half, k).start()

    for k in (0, 1):
        r_send(k).start()
    for half in (0, 1):
        z_send(1, half).start()

        @pl.when(middle)
        def _():
            z_send(2, half).start()

        for k, (sd, way) in enumerate(kinds):
            at = (rows(half), side(sd))
            remote(vec.at[at], vbuf.at[(own, *at)], v_out, x_in.at[0, half, k], dev(x_=rot(x, way))).start()
    for m in range(4):
        a_local(block_of(0, m)).start()
        a_remote(block_of(0, m)).start()
    pl.semaphore_wait(word.at[0], 6)
    tell(word.at[1], rounds[1])
    @pl.loop(4, 16)
    def _(m):
        n = block_of(m // 4, lax.rem(m, 4))
        a_local(n).start()
        a_remote(n).start()

    acc[...] = jnp.zeros_like(acc)

    def project(n):
        a_local(n).wait()
        a_remote(n).wait_recv()
        a_hi, a_lo = halves(abuf[:, n].reshape(128, 512))
        v_hi, v_lo = halves(vbuf[n])
        acc[...] += lax.dot_general(
            jnp.concatenate([a_hi, a_lo], 0), jnp.concatenate([v_hi, v_lo], 0), NT, preferred_element_type=F32
        )

    def relay(i):
        for half in (0, 1):
            for k in (0, 1):
                x_send(i, half, k).wait_recv()
                x_relay(i, half, k).start()

    def near(i):
        project(block_of(i, 0))
        for k in (2, 3):
            for half in (0, 1):
                x_send(i, half, k).wait_recv()
            project(block_of(i, (-1, 1)[k - 2]))

    def far(i):
        for half in (0, 1):
            for k in (0, 1):
                x_relay(i, half, k).wait_recv()
        project(block_of(i, 2))

    for k in (0, 1):
        r_send(k).wait_recv()
        r_relay(k).start()
    c_sends = [
        remote(cbuf.at[zl], cbuf.at[zl], c_out, c_in.at[d - 1], dev(zl_=rot(zl, d))) for d in (1, 2, 3)
    ]

    def maps():
        first = lax.broadcasted_iota(jnp.int32, (32, 128), 1) < 64
        for p in range(4):
            v = rbuf[:, p, :]
            swapped = pltpu.roll(v, 64, 1)
            for par in range(2):
                low, high = (v, swapped) if par == 0 else (swapped, v)
                rwide[p, pl.ds(par, 32, stride=2)] = jnp.where(first, low, 0.0)
                rwide[p, pl.ds(64 + par, 32, stride=2)] = jnp.where(first, 0.0, high)
            hi, lo = halves(rwide[p])
            for k, w in enumerate((hi, hi, lo)):
                rcat[k * 128 : k * 128 + 128, p * 128 : p * 128 + 128] = w
        bcat[...] = jnp.zeros_like(bcat)
        for d in (1, 2, 3):
            c_sends[d - 1].wait_recv()
        for k in range(4):
            for q in range(2):
                hi, lo = halves(cbuf[k, :, q, :])
                ccat[k * 64 + q * 32 : k * 64 + q * 32 + 32] = jnp.concatenate([hi, lo, hi], 1)

    pltpu.make_async_copy(vec, vbuf.at[own], v_in).wait()

    @pl.loop(1, 4)
    def _(i):
        edge = jnp.logical_not(middle)

        @pl.when(jnp.logical_or(i == 1, edge))
        def _():
            for half in (0, 1):
                z_take(i, half)

        @pl.when(jnp.logical_and(i < 3, middle))
        def _():
            for half in (0, 1):
                z_take(i + 1, half)

        @pl.when(i == 1)
        def _():
            relay(0)
            for k in (0, 1):
                r_relay(k).wait_recv()
            b_copy(zl, row_of(1)).start()

            @pl.when(middle)
            def _():
                b_copy(zl, row_of(2)).start()

            near(0)

        @pl.when(i > 1)
        def _():
            relay(i - 1)

        @pl.when(jnp.logical_or(i == 2, jnp.logical_and(i == 3, edge)))
        def _():
            b_take(i - 1)

        @pl.when(jnp.logical_and(i > 1, middle))
        def _():
            b_take(i)

        @pl.when(jnp.logical_and(i == 3, middle))
        def _():
            relay(3)

        @pl.when(i == 2)
        def _():
            far(0)
            pl.semaphore_wait(word.at[1], 3)
            tell(word.at[2], rounds[2])

        @pl.when(i == 3)
        def _():
            near(1)
            near(2)

    @pl.when(jnp.logical_not(middle))
    def _():
        relay(3)
        b_take(3)

    far(1)
    for copy in map_copies:
        copy.wait()
    for copy in c_sends:
        copy.start()
    near(3)
    far(2)
    far(3)

    both = acc[:128] + acc[128:]
    both = both + pltpu.roll(both, 64, 1)
    first = lax.broadcasted_iota(jnp.int32, (32, 128), 1) < 64
    for s in range(2):
        part[s * 32 : s * 32 + 32] = jnp.where(first, both[s * 64 : s * 64 + 32], both[s * 64 + 32 : s * 64 + 64])

    pl.semaphore_wait(word.at[2], 5)
    mine = y * 2 + core

    def eighth(k):
        return pl.ds(pl.multiple_of(k * 8, 8), 8)

    def scatter(k):
        to = lax.rem(mine + k, 8)
        return remote(part.at[eighth(to)], piece8.at[mine], p8_out, p8_in.at[k - 1], dev(y_=to // 2, core_=lax.rem(to, 2)))

    for k in (5, 4, 3, 2, 6, 7, 1):
        scatter(k).start()
    piece8[mine] = part[eighth(mine)]
    for k in range(1, 8):
        scatter(k).wait_recv()
    piece4[zh] = jnp.sum(piece8[...], axis=0)

    def spread(d):
        return remote(piece4.at[zh], piece4.at[zh], p4_out, p4_in.at[d - 1], dev(zh_=rot(zh, d)))

    for d in (2, 1, 3):
        spread(d).start()
    maps()
    for d in (1, 2, 3):
        spread(d).wait_recv()
    here = pl.ds(pl.multiple_of(x * 64 + mine * 8, 8), 8)
    slabs[here] = jnp.sum(piece4[...], axis=0)

    for dx in (2, 1, 3, 0):
        for dy in (2, 1, 3, 0):
            for core_ in (1 - core, core):
                if dx or dy or core_ is not core:
                    to = dev(x_=rot(x, dx), y_=rot(y, dy), core_=core_)
                    remote(slabs.at[here], slabs.at[here], s_out, s_in, to).start()

    drain(slabs.at[pl.ds(0, 248)], s_in)

    lhs = jnp.concatenate(
        [slabs[pl.ds(t * 128 + par, 32, stride=2)] for t in range(2) for par in range(2)], 0
    )
    l_hi, l_lo = halves(lhs)
    gbuf[...] = lax.dot_general(
        jnp.concatenate([l_hi, l_lo, l_hi], 1), rcat[...], NN, preferred_element_type=F32
    )
    for p in range(4):
        cols = slice(p * 128, p * 128 + 128)
        gswap[:, cols] = pltpu.roll(gbuf[:, cols], 64, 1)
    for t in range(2):
        b_hi, b_lo = halves(slabs[t * 128 + 64 : t * 128 + 128])
        for k, v in enumerate((b_hi, b_hi, b_lo)):
            for par in range(2):
                bcat[t, k * 128 + par * 64 : k * 128 + par * 64 + 64, par * 128 : par * 128 + 128] = v
        hbuf[t] = lax.dot_general(ccat[...], bcat[t], NN, preferred_element_type=F32)

    row = lax.broadcasted_iota(jnp.int32, (8, 128), 0)
    lane = lax.broadcasted_iota(jnp.int32, (8, 128), 1)

    def rows_of_sums(parts):
        for shift in (1, 2, 4):
            even = row % (2 * shift) < shift
            parts = [
                jnp.where(even, a, b) + pltpu.roll(jnp.where(even, b, a), shift, 0)
                for a, b in zip(parts[::2], parts[1::2])
            ]
        return parts[0]

    @pl.loop(0, 4)
    def _(to):
        totals = [None, None]
        for t in range(2):
            h = [
                [
                    hbuf[t, pl.ds(pl.multiple_of(to * 64 + q * 32 + k * 8, 8), 8), par * 128 : par * 128 + 128]
                    for par in range(2)
                    for k in range(4)
                ]
                for q in range(2)
            ]
            for z, g_ref in enumerate((gbuf, gswap)):
                parts = []
                for p in range(4):
                    g = [g_ref[t * 64 + k * 8 : t * 64 + k * 8 + 8, p * 128 : p * 128 + 128] for k in range(8)]
                    for q in range(2):
                        terms = [a * b for a, b in zip(g, h[q])]
                        parts.append(functools.reduce(jnp.add, terms))
                v = rows_of_sums(parts)
                v = jnp.where(lane < 64, v, -v) if z == 0 else v
                v = jnp.where(lane == zl * 2 + t, jnp.sum(v, axis=1, keepdims=True), 0.0)
                totals[z] = v if totals[z] is None else totals[z] + v
        for z in range(2):
            msg[to, z * 8 : z * 8 + 8] = totals[z]

    def answer(d):
        return remote(msg.at[rot(zl, d)], res.at[zl], m_out, m_in.at[d - 1], dev(zl_=rot(zl, d)))

    for d in (1, 2, 3):
        answer(d).start()
    res[zl] = msg[zl]
    for d in (1, 2, 3):
        answer(d).wait_recv()
    out[...] = jnp.sum(res[...], axis=0)[:, :8]

    drain(vbuf.at[pl.ds(0, 14), pl.ds(0, 56)], v_out)

    @pl.when(middle)
    def _():
        drain(vbuf.at[pl.ds(0, 11), pl.ds(0, 32)], v_out)

    drain(abuf.at[0], a_rout)
    drain(cbuf.at[pl.ds(0, 3)], c_out)
    drain(piece8.at[pl.ds(0, 7)], p8_out)
    drain(piece4.at[pl.ds(0, 3)], p4_out)
    drain(slabs.at[pl.ds(0, 248)], s_out)
    drain(res.at[pl.ds(0, 3)], m_out)


def local(amplitudes, vectors, row_map, col_map):
    dma = pltpu.SemaphoreType.DMA
    got = pl.pallas_call(
        kernel,
        out_shape=jax.ShapeDtypeStruct((16, 8), F32),
        in_specs=[pl.BlockSpec(memory_space=pl.ANY)] * 4,
        out_specs=pl.BlockSpec(memory_space=pltpu.VMEM),
        scratch_shapes=[
            pltpu.VMEM((2, 16, 64, 512), F32),
            pltpu.VMEM((16, 64, 512), F32),
            pltpu.VMEM((32, 4, 128), F32),
            pltpu.VMEM((4, 32, 2, 128), F32),
            pltpu.VMEM((256, 128), F32),
            pltpu.VMEM((64, 128), F32),
            pltpu.VMEM((8, 8, 128), F32),
            pltpu.VMEM((4, 8, 128), F32),
            pltpu.VMEM((256, 128), F32),
            pltpu.VMEM((4, 128, 128), F32),
            pltpu.VMEM((384, 512), BF16),
            pltpu.VMEM((256, 384), BF16),
            pltpu.VMEM((2, 384, 256), BF16),
            pltpu.VMEM((128, 512), F32),
            pltpu.VMEM((128, 512), F32),
            pltpu.VMEM((2, 256, 256), F32),
            pltpu.VMEM((4, 16, 128), F32),
            pltpu.VMEM((4, 16, 128), F32),
            dma((16,)), dma((16,)), dma, dma, dma((4, 2)), dma((4,)), dma((4,)), dma((4, 2, 6)), dma, dma((2,)), dma((3,)), dma,
            dma((7,)), dma, dma((3,)), dma, dma, dma, dma((3,)), dma, pltpu.SemaphoreType.REGULAR((3,)),
        ],
        compiler_params=pltpu.CompilerParams(collective_id=0, has_side_effects=True),
    )(
        amplitudes.reshape(64, -1),
        vectors,
        row_map.reshape(4, 32, 128).transpose(1, 0, 2),
        col_map.reshape(2, 32, 128).transpose(1, 0, 2),
    )
    return got.reshape(2, 4, 2, 8).transpose(0, 3, 1, 2)


def solution(mesh):
    return jax.shard_map(
        local,
        mesh=mesh,
        in_specs=(
            P(None, "bond", "leg"),
            P(None, ("leg", "bond")),
            P("leg", None),
            P("bond", None),
        ),
        out_specs=P(None, None, "leg", "bond"),
        check_vma=False,
    )
```

```python
import functools

import jax
import jax.numpy as jnp
from jax import lax
from jax.experimental import pallas as pl
from jax.experimental.pallas import tpu as pltpu
from jax.sharding import PartitionSpec as P

MESH = pl.DeviceIdType.MESH
F32, BF16 = jnp.float32, jnp.bfloat16
NT = (((1,), (1,)), ((), ()))
NN = (((1,), (0,)), ((), ()))


def halves(v):
    hi = v.astype(BF16)
    return hi, (v - hi.astype(F32)).astype(BF16)


def kernel(
    amp, vec, rmap, cmap, out,
    abuf, vbuf, rbuf, cbuf, acc, part, piece8, piece4, slabs, rwide, rcat, ccat, bcat, gbuf, gswap, hbuf, msg, res,
    a_in, a_rin, a_rout, v_in, z_in, b_in, r_in, x_in, v_out, r_out, map_in, c_in, c_out,
    p8_in, p8_out, p4_in, p4_out, s_in, s_out, m_in, m_out, word,
):
    bond, leg = lax.axis_index("bond"), lax.axis_index("leg")
    core, x, zl = lax.rem(bond, 2), lax.rem(bond // 2, 4), bond // 8
    y, zh = lax.rem(leg, 4), leg // 4

    def dev(x_=x, zl_=zl, core_=core, y_=y, zh_=zh):
        return ((zl_ * 4 + x_) * 2 + core_, zh_ * 4 + y_)

    def rot(v, d):
        return lax.rem(v + (d + 4), 4)

    def remote(src, dst, send, recv, device):
        return pltpu.make_async_remote_copy(
            src_ref=src, dst_ref=dst, send_sem=send, recv_sem=recv, device_id=device, device_id_type=MESH
        )

    def drain(ref, sem):
        pltpu.make_async_copy(ref, ref, sem).wait()

    def up(d):
        z_ = lax.rem(zh * 4 + zl + (d + 16), 16)
        return dev(zl_=lax.rem(z_, 4), zh_=z_ // 4)

    beside = [dev(x_=rot(x, d)) for d in (1, -1)] + [dev(y_=rot(y, d)) for d in (1, -1)] + [up(1), up(-1)]
    partner = dev(core_=1 - core)
    rounds = (beside, [partner, up(2), up(-2)], [dev(y_=rot(y, d)) for d in (1, 2, 3)] + [up(4), up(-4)])

    def tell(sem, devices):
        for device in devices:
            pl.semaphore_signal(sem, inc=1, device_id=device, device_id_type=MESH)

    barrier = pltpu.get_barrier_semaphore()
    tell(barrier, beside + [partner])

    own = zl * 4 + x
    pltpu.make_async_copy(vec, vbuf.at[own], v_in).start()
    map_copies = (pltpu.make_async_copy(rmap, rbuf, map_in.at[0]), pltpu.make_async_copy(cmap, cbuf.at[zl], map_in.at[1]))
    for copy in map_copies:
        copy.start()

    def row_of(i):
        low, odd = zl < 2, lax.rem(zl, 2) == 1
        first = jnp.where(odd, 2, 1)
        second = jnp.where(odd, jnp.where(low, 0, 1), jnp.where(low, 2, 3))
        third = jnp.where(low, 3, 0)
        return jnp.where(i == 0, zl, jnp.where(i == 1, first, jnp.where(i == 2, second, third)))

    def block_of(i, xo):
        return row_of(i) * 4 + rot(x, xo)

    def a_local(n):
        cols = pl.ds(pl.multiple_of((n * 2 + core) * 512, 512), 512)
        return pltpu.make_async_copy(amp.at[:, cols], abuf.at[core, n], a_in.at[n])

    def a_remote(n):
        cols = pl.ds(pl.multiple_of((n * 2 + 1 - core) * 512, 512), 512)
        return remote(amp.at[:, cols], abuf.at[core, n], a_rout, a_rin.at[n], dev(core_=1 - core))

    pl.semaphore_wait(barrier, 7)
    tell(word.at[0], rounds[0])

    rest = pl.ds(56, 8)

    def rows(half):
        return (pl.ds(0, 32), pl.ds(32, 24))[half]

    def side(k):
        return pl.ds(k * 256, 256)

    kinds = ((0, 1), (1, -1), (1, 1), (0, -1))

    def x_send(i, half, k):
        ref = vbuf.at[block_of(i, 0), rows(half), side(kinds[k][0])]
        return remote(ref, ref, v_out, x_in.at[i, half, k], dev(x_=rot(x, kinds[k][1])))

    def x_relay(i, half, k):
        ref = vbuf.at[block_of(i, -kinds[k][1]), rows(half), side(kinds[k][0])]
        return remote(ref, ref, v_out, x_in.at[i, half, 4 + k], dev(x_=rot(x, kinds[k][1])))

    def r_send(k):
        return remote(vec.at[rest], vbuf.at[own, rest], r_out, r_in.at[k], dev(x_=rot(x, kinds[k][1])))

    def r_relay(k):
        ref = vbuf.at[zl * 4 + rot(x, -kinds[k][1]), rest, side(k)]
        return remote(ref, ref, r_out, r_in.at[2 + k], dev(x_=rot(x, kinds[k][1])))

    middle = jnp.logical_and(zl > 0, zl < 3)

    def b_send(i):
        ref = vbuf.at[pl.ds(zl * 4, 4), rest]
        return remote(ref, ref, r_out, b_in.at[zl], dev(zl_=row_of(i)))

    def b_take(i):
        ref = vbuf.at[pl.ds(row_of(i) * 4, 4), rest]
        remote(ref, ref, r_out, b_in.at[row_of(i)], dev()).wait_recv()

    def z_send(i, half):
        return remote(vec.at[rows(half)], vbuf.at[own, rows(half)], v_out, z_in.at[zl, half], dev(zl_=row_of(i)))

    def z_take(i, half):
        r = row_of(i)
        ref = vbuf.at[r * 4 + x, rows(half)]
        copy = remote(ref, ref, v_out, z_in.at[r, half], dev(zl_=jnp.where(r > zl, zl - 1, zl + 1)))
        copy.wait_recv()

        @pl.when(middle)
        def _():
            copy.start()

        for k in range(4):
            x_send(i, half, k).start()

    for k in (0, 1):
        r_send(k).start()
    for half in (0, 1):
        z_send(1, half).start()

        @pl.when(middle)
        def _():
            z_send(2, half).start()

        for k, (sd, way) in enumerate(kinds):
            at = (rows(half), side(sd))
            remote(vec.at[at], vbuf.at[(own, *at)], v_out, x_in.at[0, half, k], dev(x_=rot(x, way))).start()
    for m in range(4):
        a_local(block_of(0, m)).start()
        a_remote(block_of(0, m)).start()
    pl.semaphore_wait(word.at[0], 6)
    tell(word.at[1], rounds[1])
    @pl.loop(4, 16)
    def _(m):
        n = block_of(m // 4, lax.rem(m, 4))
        a_local(n).start()
        a_remote(n).start()

    acc[...] = jnp.zeros_like(acc)

    def project(n):
        a_local(n).wait()
        a_remote(n).wait_recv()
        a_hi, a_lo = halves(abuf[:, n].reshape(128, 512))
        v_hi, v_lo = halves(vbuf[n])
        acc[...] += lax.dot_general(
            jnp.concatenate([a_hi, a_lo], 0), jnp.concatenate([v_hi, v_lo], 0), NT, preferred_element_type=F32
        )

    def relay(i):
        for half in (0, 1):
            for k in (0, 1):
                x_send(i, half, k).wait_recv()
                x_relay(i, half, k).start()

    def near(i):
        project(block_of(i, 0))
        for k in (2, 3):
            for half in (0, 1):
                x_send(i, half, k).wait_recv()
            project(block_of(i, (-1, 1)[k - 2]))

    def far(i):
        for half in (0, 1):
            for k in (0, 1):
                x_relay(i, half, k).wait_recv()
        project(block_of(i, 2))

    for k in (0, 1):
        r_send(k).wait_recv()
        r_relay(k).start()
    c_sends = [
        remote(cbuf.at[zl], cbuf.at[zl], c_out, c_in.at[d - 1], dev(zl_=rot(zl, d))) for d in (1, 2, 3)
    ]

    def maps():
        first = lax.broadcasted_iota(jnp.int32, (32, 128), 1) < 64
        for p in range(4):
            v = rbuf[:, p, :]
            swapped = pltpu.roll(v, 64, 1)
            for par in range(2):
                low, high = (v, swapped) if par == 0 else (swapped, v)
                rwide[p, pl.ds(par, 32, stride=2)] = jnp.where(first, low, 0.0)
                rwide[p, pl.ds(64 + par, 32, stride=2)] = jnp.where(first, 0.0, high)
            hi, lo = halves(rwide[p])
            for k, w in enumerate((hi, hi, lo)):
                rcat[k * 128 : k * 128 + 128, p * 128 : p * 128 + 128] = w
        bcat[...] = jnp.zeros_like(bcat)
        for d in (1, 2, 3):
            c_sends[d - 1].wait_recv()
        for k in range(4):
            for q in range(2):
                hi, lo = halves(cbuf[k, :, q, :])
                ccat[k * 64 + q * 32 : k * 64 + q * 32 + 32] = jnp.concatenate([hi, lo, hi], 1)

    pltpu.make_async_copy(vec, vbuf.at[own], v_in).wait()

    edge = jnp.logical_not(middle)
    next_row = jnp.where(middle, 3, 2)

    z_take(1, 0)
    z_take(1, 1)

    @pl.when(middle)
    def _():
        z_take(2, 0)
        z_take(2, 1)

    relay(0)
    z_take(next_row, 0)
    for k in (0, 1):
        r_relay(k).wait_recv()
    z_take(next_row, 1)
    pl.semaphore_wait(word.at[1], 3)
    tell(word.at[2], rounds[2])
    for i in (1, 2, 3):
        b_send(i).start()
    relay(1)

    @pl.when(middle)
    def _():
        near(0)
        far(0)

    @pl.when(edge)
    def _():
        z_take(3, 0)
        z_take(3, 1)

    relay(2)

    @pl.when(middle)
    def _():
        relay(3)

    @pl.when(edge)
    def _():
        near(0)
        far(0)

    b_take(1)
    near(1)

    @pl.when(edge)
    def _():
        relay(3)

    for copy in map_copies:
        copy.wait()
    for copy in c_sends:
        copy.start()
    b_take(2)
    near(2)
    far(1)
    b_take(3)
    near(3)
    far(2)
    far(3)

    both = acc[:128] + acc[128:]
    both = both + pltpu.roll(both, 64, 1)
    first = lax.broadcasted_iota(jnp.int32, (32, 128), 1) < 64
    for s in range(2):
        part[s * 32 : s * 32 + 32] = jnp.where(first, both[s * 64 : s * 64 + 32], both[s * 64 + 32 : s * 64 + 64])

    pl.semaphore_wait(word.at[2], 5)
    mine = y * 2 + core

    def eighth(k):
        return pl.ds(pl.multiple_of(k * 8, 8), 8)

    def scatter(k):
        to = lax.rem(mine + k, 8)
        return remote(part.at[eighth(to)], piece8.at[mine], p8_out, p8_in.at[k - 1], dev(y_=to // 2, core_=lax.rem(to, 2)))

    for k in (5, 4, 3, 2, 6, 7, 1):
        scatter(k).start()
    piece8[mine] = part[eighth(mine)]
    for k in range(1, 8):
        scatter(k).wait_recv()
    piece4[zh] = jnp.sum(piece8[...], axis=0)

    def spread(d):
        return remote(piece4.at[zh], piece4.at[zh], p4_out, p4_in.at[d - 1], dev(zh_=rot(zh, d)))

    for d in (2, 1, 3):
        spread(d).start()
    maps()
    for d in (1, 2, 3):
        spread(d).wait_recv()
    here = pl.ds(pl.multiple_of(x * 64 + mine * 8, 8), 8)
    slabs[here] = jnp.sum(piece4[...], axis=0)

    for dx in (2, 1, 3, 0):
        for dy in (2, 1, 3, 0):
            for core_ in (1 - core, core):
                if dx or dy or core_ is not core:
                    to = dev(x_=rot(x, dx), y_=rot(y, dy), core_=core_)
                    remote(slabs.at[here], slabs.at[here], s_out, s_in, to).start()

    drain(slabs.at[pl.ds(0, 248)], s_in)

    lhs = jnp.concatenate(
        [slabs[pl.ds(t * 128 + par, 32, stride=2)] for t in range(2) for par in range(2)], 0
    )
    l_hi, l_lo = halves(lhs)
    gbuf[...] = lax.dot_general(
        jnp.concatenate([l_hi, l_lo, l_hi], 1), rcat[...], NN, preferred_element_type=F32
    )
    for p in range(4):
        cols = slice(p * 128, p * 128 + 128)
        gswap[:, cols] = pltpu.roll(gbuf[:, cols], 64, 1)
    for t in range(2):
        b_hi, b_lo = halves(slabs[t * 128 + 64 : t * 128 + 128])
        for k, v in enumerate((b_hi, b_hi, b_lo)):
            for par in range(2):
                bcat[t, k * 128 + par * 64 : k * 128 + par * 64 + 64, par * 128 : par * 128 + 128] = v
        hbuf[t] = lax.dot_general(ccat[...], bcat[t], NN, preferred_element_type=F32)

    row = lax.broadcasted_iota(jnp.int32, (8, 128), 0)
    lane = lax.broadcasted_iota(jnp.int32, (8, 128), 1)

    def rows_of_sums(parts):
        for shift in (1, 2, 4):
            even = row % (2 * shift) < shift
            parts = [
                jnp.where(even, a, b) + pltpu.roll(jnp.where(even, b, a), shift, 0)
                for a, b in zip(parts[::2], parts[1::2])
            ]
        return parts[0]

    for to in range(4):
        totals = [None, None]
        for t in range(2):
            h = [
                [
                    hbuf[t, pl.ds(to * 64 + q * 32 + k * 8, 8), par * 128 : par * 128 + 128]
                    for par in range(2)
                    for k in range(4)
                ]
                for q in range(2)
            ]
            for z, g_ref in enumerate((gbuf, gswap)):
                parts = []
                for p in range(4):
                    g = [g_ref[t * 64 + k * 8 : t * 64 + k * 8 + 8, p * 128 : p * 128 + 128] for k in range(8)]
                    for q in range(2):
                        terms = [a * b for a, b in zip(g, h[q])]
                        parts.append(functools.reduce(jnp.add, terms))
                v = rows_of_sums(parts)
                v = jnp.where(lane < 64, v, -v) if z == 0 else v
                v = jnp.where(lane == zl * 2 + t, jnp.sum(v, axis=1, keepdims=True), 0.0)
                totals[z] = v if totals[z] is None else totals[z] + v
        for z in range(2):
            msg[to, z * 8 : z * 8 + 8] = totals[z]

    def answer(d):
        return remote(msg.at[rot(zl, d)], res.at[zl], m_out, m_in.at[d - 1], dev(zl_=rot(zl, d)))

    for d in (1, 2, 3):
        answer(d).start()
    res[zl] = msg[zl]
    for d in (1, 2, 3):
        answer(d).wait_recv()
    out[...] = jnp.sum(res[...], axis=0)[:, :8]

    drain(vbuf.at[pl.ds(0, 13), pl.ds(0, 56)], v_out)
    drain(vbuf.at[pl.ds(0, 15), pl.ds(0, 8)], r_out)

    @pl.when(middle)
    def _():
        drain(vbuf.at[pl.ds(0, 4), pl.ds(0, 56)], v_out)

    drain(abuf.at[0], a_rout)
    drain(cbuf.at[pl.ds(0, 3)], c_out)
    drain(piece8.at[pl.ds(0, 7)], p8_out)
    drain(piece4.at[pl.ds(0, 3)], p4_out)
    drain(slabs.at[pl.ds(0, 248)], s_out)
    drain(res.at[pl.ds(0, 3)], m_out)


def local(amplitudes, vectors, row_map, col_map):
    dma = pltpu.SemaphoreType.DMA
    got = pl.pallas_call(
        kernel,
        out_shape=pltpu.VMEM((16, 8), F32),
        in_specs=[pl.BlockSpec(memory_space=pl.ANY)] * 4,
        out_specs=pl.BlockSpec(memory_space=pltpu.VMEM),
        scratch_shapes=[
            pltpu.VMEM((2, 16, 64, 512), F32),
            pltpu.VMEM((16, 64, 512), F32),
            pltpu.VMEM((32, 4, 128), F32),
            pltpu.VMEM((4, 32, 2, 128), F32),
            pltpu.VMEM((256, 128), F32),
            pltpu.VMEM((64, 128), F32),
            pltpu.VMEM((8, 8, 128), F32),
            pltpu.VMEM((4, 8, 128), F32),
            pltpu.VMEM((256, 128), F32),
            pltpu.VMEM((4, 128, 128), F32),
            pltpu.VMEM((384, 512), BF16),
            pltpu.VMEM((256, 384), BF16),
            pltpu.VMEM((2, 384, 256), BF16),
            pltpu.VMEM((128, 512), F32),
            pltpu.VMEM((128, 512), F32),
            pltpu.VMEM((2, 256, 256), F32),
            pltpu.VMEM((4, 16, 128), F32),
            pltpu.VMEM((4, 16, 128), F32),
            dma((16,)), dma((16,)), dma, dma, dma((4, 2)), dma((4,)), dma((4,)), dma((4, 2, 6)), dma, dma, dma((2,)), dma((3,)), dma,
            dma((7,)), dma, dma((3,)), dma, dma, dma, dma((3,)), dma, pltpu.SemaphoreType.REGULAR((3,)),
        ],
        compiler_params=pltpu.CompilerParams(collective_id=0, has_side_effects=True),
    )(
        amplitudes.reshape(64, -1),
        vectors,
        row_map.reshape(4, 32, 128).transpose(1, 0, 2),
        col_map.reshape(2, 32, 128).transpose(1, 0, 2),
    )
    return got.reshape(2, 4, 2, 8).transpose(0, 3, 1, 2)


def solution(mesh):
    return jax.shard_map(
        local,
        mesh=mesh,
        in_specs=(
            P(None, "bond", "leg"),
            P(None, ("leg", "bond")),
            P("leg", None),
            P("bond", None),
        ),
        out_specs=P(None, None, "leg", "bond"),
        check_vma=False,
    )
```

```python
import functools

import jax
import jax.numpy as jnp
from jax import lax
from jax.experimental import pallas as pl
from jax.experimental.pallas import tpu as pltpu
from jax.sharding import PartitionSpec as P

MESH = pl.DeviceIdType.MESH
F32, BF16 = jnp.float32, jnp.bfloat16
NT = (((1,), (1,)), ((), ()))
NN = (((1,), (0,)), ((), ()))


def halves(v):
    hi = v.astype(BF16)
    return hi, (v - hi.astype(F32)).astype(BF16)


def kernel(
    amp, vec, rmap, cmap, out,
    abuf, vbuf, rbuf, cbuf, acc, part, piece8, piece4, slabs, rwide, rcat, ccat, bcat, gbuf, gswap, hbuf, msg, res,
    a_in, a_rin, a_rout, v_in, z_in, b_in, r_in, x_in, v_out, r_out, map_in, c_in, c_out,
    p8_in, p8_out, p4_in, p4_out, s_in, s_out, m_in, m_out, word,
):
    bond, leg = lax.axis_index("bond"), lax.axis_index("leg")
    core, x, zl = lax.rem(bond, 2), lax.rem(bond // 2, 4), bond // 8
    y, zh = lax.rem(leg, 4), leg // 4

    def dev(x_=x, zl_=zl, core_=core, y_=y, zh_=zh):
        return ((zl_ * 4 + x_) * 2 + core_, zh_ * 4 + y_)

    def rot(v, d):
        return lax.rem(v + (d + 4), 4)

    def remote(src, dst, send, recv, device):
        return pltpu.make_async_remote_copy(
            src_ref=src, dst_ref=dst, send_sem=send, recv_sem=recv, device_id=device, device_id_type=MESH
        )

    def drain(ref, sem):
        pltpu.make_async_copy(ref, ref, sem).wait()

    def up(d):
        z_ = lax.rem(zh * 4 + zl + (d + 16), 16)
        return dev(zl_=lax.rem(z_, 4), zh_=z_ // 4)

    middle = jnp.logical_and(zl > 0, zl < 3)
    edge = jnp.logical_not(middle)
    first = jnp.logical_or(jnp.logical_and(zl == 3, zh < 3), jnp.logical_and(zl == 0, zh == 0))
    inward = jnp.where(zl == 3, -1, 1)
    outside = up(-inward)
    inside = up(inward)
    beside = [dev(x_=rot(x, d)) for d in (1, -1)] + [dev(y_=rot(y, d)) for d in (1, -1)]
    partner = dev(core_=1 - core)
    rounds = (beside, [partner, up(2), up(-2)], [dev(y_=rot(y, d)) for d in (1, 2, 3)] + [up(4), up(-4)])

    def tell(sem, devices):
        for device in devices:
            pl.semaphore_signal(sem, inc=1, device_id=device, device_id_type=MESH)

    barrier = pltpu.get_barrier_semaphore()
    tell(barrier, beside[:2] + [inside] + beside[2:] + [partner])

    @pl.when(jnp.logical_or(middle, first))
    def _():
        tell(barrier, [outside])

    own = zl * 4 + x
    pltpu.make_async_copy(vec, vbuf.at[own], v_in).start()
    map_copies = (pltpu.make_async_copy(rmap, rbuf, map_in.at[0]), pltpu.make_async_copy(cmap, cbuf.at[zl], map_in.at[1]))
    for copy in map_copies:
        copy.start()

    def row_of(i):
        low, odd = zl < 2, lax.rem(zl, 2) == 1
        first = jnp.where(odd, 2, 1)
        second = jnp.where(odd, jnp.where(low, 0, 1), jnp.where(low, 2, 3))
        third = jnp.where(low, 3, 0)
        return jnp.where(i == 0, zl, jnp.where(i == 1, first, jnp.where(i == 2, second, third)))

    def block_of(i, xo):
        return row_of(i) * 4 + rot(x, xo)

    def a_local(n):
        cols = pl.ds(pl.multiple_of((n * 2 + core) * 512, 512), 512)
        return pltpu.make_async_copy(amp.at[:, cols], abuf.at[core, n], a_in.at[n])

    def a_remote(n):
        cols = pl.ds(pl.multiple_of((n * 2 + 1 - core) * 512, 512), 512)
        return remote(amp.at[:, cols], abuf.at[core, n], a_rout, a_rin.at[n], dev(core_=1 - core))

    @pl.when(first)
    def _():
        pl.semaphore_wait(barrier, 6)

    @pl.when(jnp.logical_not(first))
    def _():
        pl.semaphore_wait(barrier, 7)


    rest = pl.ds(56, 8)

    def rows(half):
        return (pl.ds(0, 32), pl.ds(32, 24))[half]

    def side(k):
        return pl.ds(k * 256, 256)

    kinds = ((0, 1), (1, -1), (1, 1), (0, -1))

    def x_send(i, half, k):
        ref = vbuf.at[block_of(i, 0), rows(half), side(kinds[k][0])]
        return remote(ref, ref, v_out, x_in.at[i, half, k], dev(x_=rot(x, kinds[k][1])))

    def x_relay(i, half, k):
        ref = vbuf.at[block_of(i, -kinds[k][1]), rows(half), side(kinds[k][0])]
        return remote(ref, ref, v_out, x_in.at[i, half, 4 + k], dev(x_=rot(x, kinds[k][1])))

    def r_send(k):
        return remote(vec.at[rest], vbuf.at[own, rest], r_out, r_in.at[k], dev(x_=rot(x, kinds[k][1])))

    def r_relay(k):
        ref = vbuf.at[zl * 4 + rot(x, -kinds[k][1]), rest, side(k)]
        return remote(ref, ref, r_out, r_in.at[2 + k], dev(x_=rot(x, kinds[k][1])))

    def b_send(i):
        ref = vbuf.at[pl.ds(zl * 4, 4), rest]
        return remote(ref, ref, r_out, b_in.at[zl], dev(zl_=row_of(i)))

    def b_take(i):
        ref = vbuf.at[pl.ds(row_of(i) * 4, 4), rest]
        remote(ref, ref, r_out, b_in.at[row_of(i)], dev()).wait_recv()

    def z_send(i, half):
        return remote(vec.at[rows(half)], vbuf.at[own, rows(half)], v_out, z_in.at[zl, half], dev(zl_=row_of(i)))

    def z_take(i, half):
        r = row_of(i)
        ref = vbuf.at[r * 4 + x, rows(half)]
        copy = remote(ref, ref, v_out, z_in.at[r, half], dev(zl_=jnp.where(r > zl, zl - 1, zl + 1)))
        copy.wait_recv()

        @pl.when(middle)
        def _():
            copy.start()

        for k in range(4):
            x_send(i, half, k).start()

    for k in (0, 1):
        r_send(k).start()
    for half in (0, 1):
        z_send(1, half).start()

        @pl.when(middle)
        def _():
            z_send(2, half).start()

        for k, (sd, way) in enumerate(kinds):
            at = (rows(half), side(sd))
            remote(vec.at[at], vbuf.at[(own, *at)], v_out, x_in.at[0, half, k], dev(x_=rot(x, way))).start()
    def setup():
        tell(word.at[0], rounds[0])

        @pl.when(jnp.logical_not(first))
        def _():
            tell(word.at[0], [inside, outside])

        @pl.loop(0, 16)
        def _(m):
            n = block_of(m // 4, lax.rem(m, 4))
            a_local(n).start()
            a_remote(n).start()

    setup()
    pl.semaphore_wait(word.at[0], 6)

    @pl.when(first)
    def _():
        tell(word.at[0], [inside, outside])

    tell(word.at[1], rounds[1])
    acc[...] = jnp.zeros_like(acc)

    def project(n):
        a_local(n).wait()
        a_remote(n).wait_recv()
        a_hi, a_lo = halves(abuf[:, n].reshape(128, 512))
        v_hi, v_lo = halves(vbuf[n])
        acc[...] += lax.dot_general(
            jnp.concatenate([a_hi, a_lo], 0), jnp.concatenate([v_hi, v_lo], 0), NT, preferred_element_type=F32
        )

    def relay(i):
        for half in (0, 1):
            for k in (0, 1):
                x_send(i, half, k).wait_recv()
                x_relay(i, half, k).start()

    def near(i):
        project(block_of(i, 0))
        for k in (2, 3):
            for half in (0, 1):
                x_send(i, half, k).wait_recv()
            project(block_of(i, (-1, 1)[k - 2]))

    def far(i):
        for half in (0, 1):
            for k in (0, 1):
                x_relay(i, half, k).wait_recv()
        project(block_of(i, 2))

    for k in (0, 1):
        r_send(k).wait_recv()
        r_relay(k).start()
    c_sends = [
        remote(cbuf.at[zl], cbuf.at[zl], c_out, c_in.at[d - 1], dev(zl_=rot(zl, d))) for d in (1, 2, 3)
    ]

    def maps():
        first = lax.broadcasted_iota(jnp.int32, (32, 128), 1) < 64
        for p in range(4):
            v = rbuf[:, p, :]
            swapped = pltpu.roll(v, 64, 1)
            for par in range(2):
                low, high = (v, swapped) if par == 0 else (swapped, v)
                rwide[p, pl.ds(par, 32, stride=2)] = jnp.where(first, low, 0.0)
                rwide[p, pl.ds(64 + par, 32, stride=2)] = jnp.where(first, 0.0, high)
            hi, lo = halves(rwide[p])
            for k, w in enumerate((hi, hi, lo)):
                rcat[k * 128 : k * 128 + 128, p * 128 : p * 128 + 128] = w
        bcat[...] = jnp.zeros_like(bcat)
        for d in (1, 2, 3):
            c_sends[d - 1].wait_recv()
        for k in range(4):
            for q in range(2):
                hi, lo = halves(cbuf[k, :, q, :])
                ccat[k * 64 + q * 32 : k * 64 + q * 32 + 32] = jnp.concatenate([hi, lo, hi], 1)

    pltpu.make_async_copy(vec, vbuf.at[own], v_in).wait()

    next_row = jnp.where(middle, 3, 2)

    z_take(1, 0)
    z_take(1, 1)

    @pl.when(middle)
    def _():
        z_take(2, 0)
        z_take(2, 1)

    relay(0)
    z_take(next_row, 0)
    for k in (0, 1):
        r_relay(k).wait_recv()
    z_take(next_row, 1)
    pl.semaphore_wait(word.at[1], 3)
    tell(word.at[2], rounds[2])

    def bundles():
        for i in (1, 2, 3):
            b_send(i).start()

    pl.when(core == 0)(bundles)
    relay(1)

    @pl.when(middle)
    def _():
        near(0)
        far(0)

    @pl.when(edge)
    def _():
        z_take(3, 0)
        z_take(3, 1)

    relay(2)
    pl.when(core == 1)(bundles)

    @pl.when(middle)
    def _():
        relay(3)

    @pl.when(edge)
    def _():
        near(0)
        far(0)

    b_take(1)
    near(1)

    @pl.when(edge)
    def _():
        relay(3)

    for copy in map_copies:
        copy.wait()
    for copy in c_sends:
        copy.start()
    b_take(2)
    near(2)
    far(1)
    b_take(3)
    near(3)
    far(2)
    far(3)

    both = acc[:128] + acc[128:]
    both = both + pltpu.roll(both, 64, 1)
    first = lax.broadcasted_iota(jnp.int32, (32, 128), 1) < 64
    for s in range(2):
        part[s * 32 : s * 32 + 32] = jnp.where(first, both[s * 64 : s * 64 + 32], both[s * 64 + 32 : s * 64 + 64])

    pl.semaphore_wait(word.at[2], 5)
    mine = y * 2 + core

    def eighth(k):
        return pl.ds(pl.multiple_of(k * 8, 8), 8)

    def scatter(k):
        to = lax.rem(mine + k, 8)
        return remote(part.at[eighth(to)], piece8.at[mine], p8_out, p8_in.at[k - 1], dev(y_=to // 2, core_=lax.rem(to, 2)))

    for k in (5, 4, 3, 2, 6, 7, 1):
        scatter(k).start()
    piece8[mine] = part[eighth(mine)]
    for k in range(1, 8):
        scatter(k).wait_recv()
    piece4[zh] = jnp.sum(piece8[...], axis=0)

    def spread(d):
        return remote(piece4.at[zh], piece4.at[zh], p4_out, p4_in.at[d - 1], dev(zh_=rot(zh, d)))

    for d in (2, 1, 3):
        spread(d).start()
    maps()
    for d in (1, 2, 3):
        spread(d).wait_recv()
    here = pl.ds(pl.multiple_of(x * 64 + mine * 8, 8), 8)
    slabs[here] = jnp.sum(piece4[...], axis=0)

    for dx in (2, 1, 3, 0):
        for dy in (2, 1, 3, 0):
            for core_ in (1 - core, core):
                if dx or dy or core_ is not core:
                    to = dev(x_=rot(x, dx), y_=rot(y, dy), core_=core_)
                    remote(slabs.at[here], slabs.at[here], s_out, s_in, to).start()

    drain(slabs.at[pl.ds(0, 248)], s_in)

    lhs = jnp.concatenate(
        [slabs[pl.ds(t * 128 + par, 32, stride=2)] for t in range(2) for par in range(2)], 0
    )
    l_hi, l_lo = halves(lhs)
    gbuf[...] = lax.dot_general(
        jnp.concatenate([l_hi, l_lo, l_hi], 1), rcat[...], NN, preferred_element_type=F32
    )
    for p in range(4):
        cols = slice(p * 128, p * 128 + 128)
        gswap[:, cols] = pltpu.roll(gbuf[:, cols], 64, 1)
    for t in range(2):
        b_hi, b_lo = halves(slabs[t * 128 + 64 : t * 128 + 128])
        for k, v in enumerate((b_hi, b_hi, b_lo)):
            for par in range(2):
                bcat[t, k * 128 + par * 64 : k * 128 + par * 64 + 64, par * 128 : par * 128 + 128] = v
        hbuf[t] = lax.dot_general(ccat[...], bcat[t], NN, preferred_element_type=F32)

    row = lax.broadcasted_iota(jnp.int32, (8, 128), 0)
    lane = lax.broadcasted_iota(jnp.int32, (8, 128), 1)

    def rows_of_sums(parts):
        for shift in (1, 2, 4):
            even = row % (2 * shift) < shift
            parts = [
                jnp.where(even, a, b) + pltpu.roll(jnp.where(even, b, a), shift, 0)
                for a, b in zip(parts[::2], parts[1::2])
            ]
        return parts[0]

    for to in range(4):
        totals = [None, None]
        for t in range(2):
            h = [
                [
                    hbuf[t, pl.ds(to * 64 + q * 32 + k * 8, 8), par * 128 : par * 128 + 128]
                    for par in range(2)
                    for k in range(4)
                ]
                for q in range(2)
            ]
            for z, g_ref in enumerate((gbuf, gswap)):
                parts = []
                for p in range(4):
                    g = [g_ref[t * 64 + k * 8 : t * 64 + k * 8 + 8, p * 128 : p * 128 + 128] for k in range(8)]
                    for q in range(2):
                        terms = [a * b for a, b in zip(g, h[q])]
                        parts.append(functools.reduce(jnp.add, terms))
                v = rows_of_sums(parts)
                v = jnp.where(lane < 64, v, -v) if z == 0 else v
                v = jnp.where(lane == zl * 2 + t, jnp.sum(v, axis=1, keepdims=True), 0.0)
                totals[z] = v if totals[z] is None else totals[z] + v
        for z in range(2):
            msg[to, z * 8 : z * 8 + 8] = totals[z]

    def answer(d):
        return remote(msg.at[rot(zl, d)], res.at[zl], m_out, m_in.at[d - 1], dev(zl_=rot(zl, d)))

    for d in (1, 2, 3):
        answer(d).start()
    res[zl] = msg[zl]
    for d in (1, 2, 3):
        answer(d).wait_recv()
    out[...] = jnp.sum(res[...], axis=0)[:, :8]

    drain(vbuf.at[pl.ds(0, 13), pl.ds(0, 56)], v_out)
    drain(vbuf.at[pl.ds(0, 15), pl.ds(0, 8)], r_out)

    @pl.when(middle)
    def _():
        drain(vbuf.at[pl.ds(0, 4), pl.ds(0, 56)], v_out)

    drain(abuf.at[0], a_rout)
    drain(cbuf.at[pl.ds(0, 3)], c_out)
    drain(piece8.at[pl.ds(0, 7)], p8_out)
    drain(piece4.at[pl.ds(0, 3)], p4_out)
    drain(slabs.at[pl.ds(0, 248)], s_out)
    drain(res.at[pl.ds(0, 3)], m_out)


def local(amplitudes, vectors, row_map, col_map):
    dma = pltpu.SemaphoreType.DMA
    got = pl.pallas_call(
        kernel,
        out_shape=pltpu.VMEM((16, 8), F32),
        in_specs=[pl.BlockSpec(memory_space=pl.ANY)] * 4,
        out_specs=pl.BlockSpec(memory_space=pltpu.VMEM),
        scratch_shapes=[
            pltpu.VMEM((2, 16, 64, 512), F32),
            pltpu.VMEM((16, 64, 512), F32),
            pltpu.VMEM((32, 4, 128), F32),
            pltpu.VMEM((4, 32, 2, 128), F32),
            pltpu.VMEM((256, 128), F32),
            pltpu.VMEM((64, 128), F32),
            pltpu.VMEM((8, 8, 128), F32),
            pltpu.VMEM((4, 8, 128), F32),
            pltpu.VMEM((256, 128), F32),
            pltpu.VMEM((4, 128, 128), F32),
            pltpu.VMEM((384, 512), BF16),
            pltpu.VMEM((256, 384), BF16),
            pltpu.VMEM((2, 384, 256), BF16),
            pltpu.VMEM((128, 512), F32),
            pltpu.VMEM((128, 512), F32),
            pltpu.VMEM((2, 256, 256), F32),
            pltpu.VMEM((4, 16, 128), F32),
            pltpu.VMEM((4, 16, 128), F32),
            dma((16,)), dma((16,)), dma, dma, dma((4, 2)), dma((4,)), dma((4,)), dma((4, 2, 6)), dma, dma, dma((2,)), dma((3,)), dma,
            dma((7,)), dma, dma((3,)), dma, dma, dma, dma((3,)), dma, pltpu.SemaphoreType.REGULAR((3,)),
        ],
        compiler_params=pltpu.CompilerParams(collective_id=0, has_side_effects=True),
    )(
        amplitudes.reshape(64, -1),
        vectors,
        row_map.reshape(4, 32, 128).transpose(1, 0, 2),
        col_map.reshape(2, 32, 128).transpose(1, 0, 2),
    )
    return got.reshape(2, 4, 2, 8).transpose(0, 3, 1, 2)


def solution(mesh):
    return jax.shard_map(
        local,
        mesh=mesh,
        in_specs=(
            P(None, "bond", "leg"),
            P(None, ("leg", "bond")),
            P("leg", None),
            P("bond", None),
        ),
        out_specs=P(None, None, "leg", "bond"),
        check_vma=False,
    )
```

```python
import functools

import jax
import jax.numpy as jnp
from jax import lax
from jax.experimental import pallas as pl
from jax.experimental.pallas import tpu as pltpu
from jax.sharding import PartitionSpec as P

MESH = pl.DeviceIdType.MESH
F32, BF16 = jnp.float32, jnp.bfloat16
NT = (((1,), (1,)), ((), ()))
NN = (((1,), (0,)), ((), ()))


def halves(v):
    hi = v.astype(BF16)
    return hi, (v - hi.astype(F32)).astype(BF16)


def kernel(
    amp, vec, rmap, cmap, out,
    abuf, vbuf, rbuf, cbuf, acc, part, piece8, piece4, slabs, rwide, rcat, ccat, bcat, gbuf, gswap, hbuf, msg, res,
    a_in, a_rin, a_rout, v_in, z_in, b_in, r_in, x_in, v_out, r_out, map_in, c_in, c_out,
    p8_in, p8_out, p4_in, p4_out, s_in, s_out, m_in, m_out, word,
):
    bond, leg = lax.axis_index("bond"), lax.axis_index("leg")
    core, x, zl = lax.rem(bond, 2), lax.rem(bond // 2, 4), bond // 8
    y, zh = lax.rem(leg, 4), leg // 4

    def dev(x_=x, zl_=zl, core_=core, y_=y, zh_=zh):
        return ((zl_ * 4 + x_) * 2 + core_, zh_ * 4 + y_)

    def rot(v, d):
        return lax.rem(v + (d + 4), 4)

    def remote(src, dst, send, recv, device):
        return pltpu.make_async_remote_copy(
            src_ref=src, dst_ref=dst, send_sem=send, recv_sem=recv, device_id=device, device_id_type=MESH
        )

    def drain(ref, sem):
        pltpu.make_async_copy(ref, ref, sem).wait()

    def up(d):
        z_ = lax.rem(zh * 4 + zl + (d + 16), 16)
        return dev(zl_=lax.rem(z_, 4), zh_=z_ // 4)

    middle = jnp.logical_and(zl > 0, zl < 3)
    edge = jnp.logical_not(middle)
    first = jnp.logical_or(jnp.logical_and(zl == 3, zh < 3), jnp.logical_and(zl == 0, zh == 0))
    inward = jnp.where(zl == 3, -1, 1)
    outside = up(-inward)
    inside = up(inward)
    beside = [dev(x_=rot(x, d)) for d in (1, -1)] + [dev(y_=rot(y, d)) for d in (1, -1)]
    partner = dev(core_=1 - core)
    rounds = (beside, [partner, up(2), up(-2)], [dev(y_=rot(y, d)) for d in (1, 2, 3)] + [up(4), up(-4)])

    def tell(sem, devices):
        for device in devices:
            pl.semaphore_signal(sem, inc=1, device_id=device, device_id_type=MESH)

    barrier = pltpu.get_barrier_semaphore()
    tell(barrier, beside[:2] + [inside] + beside[2:] + [partner])

    @pl.when(jnp.logical_or(middle, first))
    def _():
        tell(barrier, [outside])

    own = zl * 4 + x
    pltpu.make_async_copy(vec, vbuf.at[own], v_in).start()
    map_copies = (pltpu.make_async_copy(rmap, rbuf, map_in.at[0]), pltpu.make_async_copy(cmap, cbuf.at[zl], map_in.at[1]))
    for copy in map_copies:
        copy.start()

    def row_of(i):
        low, odd = zl < 2, lax.rem(zl, 2) == 1
        first = jnp.where(odd, 2, 1)
        second = jnp.where(odd, jnp.where(low, 0, 1), jnp.where(low, 2, 3))
        third = jnp.where(low, 3, 0)
        return jnp.where(i == 0, zl, jnp.where(i == 1, first, jnp.where(i == 2, second, third)))

    def block_of(i, xo):
        return row_of(i) * 4 + rot(x, xo)

    def a_local(n):
        cols = pl.ds(pl.multiple_of((n * 2 + core) * 512, 512), 512)
        return pltpu.make_async_copy(amp.at[:, cols], abuf.at[core, n], a_in)

    def a_remote(n):
        cols = pl.ds(pl.multiple_of((n * 2 + 1 - core) * 512, 512), 512)
        return remote(amp.at[:, cols], abuf.at[core, n], a_rout, a_rin, dev(core_=1 - core))

    @pl.when(first)
    def _():
        pl.semaphore_wait(barrier, 6)

    @pl.when(jnp.logical_not(first))
    def _():
        pl.semaphore_wait(barrier, 7)


    rest = pl.ds(56, 8)

    def rows(half):
        return (pl.ds(0, 32), pl.ds(32, 24))[half]

    def side(k):
        return pl.ds(k * 256, 256)

    kinds = ((0, 1), (1, -1), (1, 1), (0, -1))

    def x_sem(i, half, k):
        return x_in.at[i, half * 2 + k if k < 2 else k + 2]

    def x_send(i, half, k):
        ref = vbuf.at[block_of(i, 0), rows(half), side(kinds[k][0])]
        return remote(ref, ref, v_out, x_sem(i, half, k), dev(x_=rot(x, kinds[k][1])))

    def x_relay(i, half, k):
        ref = vbuf.at[block_of(i, -kinds[k][1]), rows(half), side(kinds[k][0])]
        return remote(ref, ref, v_out, x_in.at[i, 6], dev(x_=rot(x, kinds[k][1])))

    def r_send(k):
        return remote(vec.at[rest], vbuf.at[own, rest], r_out, r_in.at[k], dev(x_=rot(x, kinds[k][1])))

    def r_relay(k):
        ref = vbuf.at[zl * 4 + rot(x, -kinds[k][1]), rest, side(k)]
        return remote(ref, ref, r_out, r_in.at[2], dev(x_=rot(x, kinds[k][1])))

    def b_send(i):
        ref = vbuf.at[pl.ds(zl * 4, 4), rest]
        return remote(ref, ref, r_out, b_in.at[zl], dev(zl_=row_of(i)))

    def b_take(i):
        ref = vbuf.at[pl.ds(row_of(i) * 4, 4), rest]
        remote(ref, ref, r_out, b_in.at[row_of(i)], dev()).wait_recv()

    def z_send(i, half):
        return remote(vec.at[rows(half)], vbuf.at[own, rows(half)], v_out, z_in.at[zl, half], dev(zl_=row_of(i)))

    def z_take(i, half):
        r = row_of(i)
        ref = vbuf.at[r * 4 + x, rows(half)]
        copy = remote(ref, ref, v_out, z_in.at[r, half], dev(zl_=jnp.where(r > zl, zl - 1, zl + 1)))
        copy.wait_recv()

        @pl.when(middle)
        def _():
            copy.start()

        for k in range(4):
            x_send(i, half, k).start()

    for k in (0, 1):
        r_send(k).start()
    for half in (0, 1):
        z_send(1, half).start()

        @pl.when(middle)
        def _():
            z_send(2, half).start()

        for k, (sd, way) in enumerate(kinds):
            at = (rows(half), side(sd))
            remote(vec.at[at], vbuf.at[(own, *at)], v_out, x_sem(0, half, k), dev(x_=rot(x, way))).start()
    def setup():
        tell(word.at[0], rounds[0])

        @pl.when(jnp.logical_not(first))
        def _():
            tell(word.at[0], [inside, outside])

        @pl.loop(0, 16)
        def _(m):
            n = block_of(m // 4, lax.rem(m, 4))
            a_local(n).start()
            a_remote(n).start()

    setup()
    pl.semaphore_wait(word.at[0], 6)

    @pl.when(first)
    def _():
        tell(word.at[0], [inside, outside])

    tell(word.at[1], rounds[1])
    acc[...] = jnp.zeros_like(acc)

    def project(n):
        a_hi, a_lo = halves(abuf[:, n].reshape(128, 512))
        v_hi, v_lo = halves(vbuf[n])
        acc[...] += lax.dot_general(
            jnp.concatenate([a_hi, a_lo], 0), jnp.concatenate([v_hi, v_lo], 0), NT, preferred_element_type=F32
        )

    def relay(i):
        for half in (0, 1):
            for k in (0, 1):
                x_send(i, half, k).wait_recv()
                x_relay(i, half, k).start()

    def near(i):
        project(block_of(i, 0))
        for k, n in ((2, block_of(i, -1)), (3, block_of(i, 1))):
            drain(vbuf.at[n, pl.ds(0, 56), side(kinds[k][0])], x_sem(i, 0, k))
            project(n)

    def far(i):
        n = block_of(i, 2)
        drain(vbuf.at[n, pl.ds(0, 56)], x_in.at[i, 6])
        project(n)

    for k in (0, 1):
        r_send(k).wait_recv()
        r_relay(k).start()
    c_sends = [
        remote(cbuf.at[zl], cbuf.at[zl], c_out, c_in, dev(zl_=rot(zl, d))) for d in (1, 2, 3)
    ]

    def maps():
        first = lax.broadcasted_iota(jnp.int32, (32, 128), 1) < 64
        for p in range(4):
            v = rbuf[:, p, :]
            swapped = pltpu.roll(v, 64, 1)
            for par in range(2):
                low, high = (v, swapped) if par == 0 else (swapped, v)
                rwide[p, pl.ds(par, 32, stride=2)] = jnp.where(first, low, 0.0)
                rwide[p, pl.ds(64 + par, 32, stride=2)] = jnp.where(first, 0.0, high)
            hi, lo = halves(rwide[p])
            for k, w in enumerate((hi, hi, lo)):
                rcat[k * 128 : k * 128 + 128, p * 128 : p * 128 + 128] = w
        bcat[...] = jnp.zeros_like(bcat)
        drain(cbuf.at[pl.ds(0, 3)], c_in)
        for k in range(4):
            for q in range(2):
                hi, lo = halves(cbuf[k, :, q, :])
                ccat[k * 64 + q * 32 : k * 64 + q * 32 + 32] = jnp.concatenate([hi, lo, hi], 1)

    pltpu.make_async_copy(vec, vbuf.at[own], v_in).wait()

    next_row = jnp.where(middle, 3, 2)

    z_take(1, 0)
    z_take(1, 1)

    @pl.when(middle)
    def _():
        z_take(2, 0)
        z_take(2, 1)

    relay(0)
    z_take(next_row, 0)
    drain(vbuf.at[own, rest], r_in.at[2])
    z_take(next_row, 1)
    pl.semaphore_wait(word.at[1], 3)
    tell(word.at[2], rounds[2])

    def bundles():
        for i in (1, 2, 3):
            b_send(i).start()

    pl.when(core == 0)(bundles)
    relay(1)
    drain(abuf.at[core], a_in)
    drain(abuf.at[1 - core], a_rin)

    @pl.when(middle)
    def _():
        near(0)
        far(0)

    @pl.when(edge)
    def _():
        z_take(3, 0)
        z_take(3, 1)

    relay(2)
    pl.when(core == 1)(bundles)

    @pl.when(middle)
    def _():
        relay(3)

    @pl.when(edge)
    def _():
        near(0)
        far(0)

    b_take(1)
    near(1)

    @pl.when(edge)
    def _():
        relay(3)

    for copy in map_copies:
        copy.wait()
    for copy in c_sends:
        copy.start()
    b_take(2)
    near(2)
    far(1)
    b_take(3)
    near(3)
    far(2)
    far(3)

    both = acc[:128] + acc[128:]
    both = both + pltpu.roll(both, 64, 1)
    first = lax.broadcasted_iota(jnp.int32, (32, 128), 1) < 64
    for s in range(2):
        part[s * 32 : s * 32 + 32] = jnp.where(first, both[s * 64 : s * 64 + 32], both[s * 64 + 32 : s * 64 + 64])

    pl.semaphore_wait(word.at[2], 5)
    mine = y * 2 + core

    def eighth(k):
        return pl.ds(pl.multiple_of(k * 8, 8), 8)

    def scatter(k):
        to = lax.rem(mine + k, 8)
        return remote(part.at[eighth(to)], piece8.at[mine], p8_out, p8_in, dev(y_=to // 2, core_=lax.rem(to, 2)))

    for k in (5, 4, 3, 2, 6, 7, 1):
        scatter(k).start()
    piece8[mine] = part[eighth(mine)]
    drain(piece8.at[pl.ds(0, 7)], p8_in)
    piece4[zh] = jnp.sum(piece8[...], axis=0)

    def spread(d):
        return remote(piece4.at[zh], piece4.at[zh], p4_out, p4_in, dev(zh_=rot(zh, d)))

    for d in (2, 1, 3):
        spread(d).start()
    maps()
    drain(piece4.at[pl.ds(0, 3)], p4_in)
    here = pl.ds(pl.multiple_of(x * 64 + mine * 8, 8), 8)
    slabs[here] = jnp.sum(piece4[...], axis=0)

    for dx in (2, 1, 3, 0):
        for dy in (2, 1, 3, 0):
            for core_ in (1 - core, core):
                if dx or dy or core_ is not core:
                    to = dev(x_=rot(x, dx), y_=rot(y, dy), core_=core_)
                    remote(slabs.at[here], slabs.at[here], s_out, s_in, to).start()

    drain(slabs.at[pl.ds(0, 248)], s_in)

    lhs = jnp.concatenate(
        [slabs[pl.ds(t * 128 + par, 32, stride=2)] for t in range(2) for par in range(2)], 0
    )
    l_hi, l_lo = halves(lhs)
    gbuf[...] = lax.dot_general(
        jnp.concatenate([l_hi, l_lo, l_hi], 1), rcat[...], NN, preferred_element_type=F32
    )
    for p in range(4):
        cols = slice(p * 128, p * 128 + 128)
        gswap[:, cols] = pltpu.roll(gbuf[:, cols], 64, 1)
    for t in range(2):
        b_hi, b_lo = halves(slabs[t * 128 + 64 : t * 128 + 128])
        for k, v in enumerate((b_hi, b_hi, b_lo)):
            for par in range(2):
                bcat[t, k * 128 + par * 64 : k * 128 + par * 64 + 64, par * 128 : par * 128 + 128] = v
        hbuf[t] = lax.dot_general(ccat[...], bcat[t], NN, preferred_element_type=F32)

    row = lax.broadcasted_iota(jnp.int32, (8, 128), 0)
    lane = lax.broadcasted_iota(jnp.int32, (8, 128), 1)

    def rows_of_sums(parts):
        for shift in (1, 2, 4):
            even = row % (2 * shift) < shift
            parts = [
                jnp.where(even, a, b) + pltpu.roll(jnp.where(even, b, a), shift, 0)
                for a, b in zip(parts[::2], parts[1::2])
            ]
        return parts[0]

    for to in range(4):
        totals = [None, None]
        for t in range(2):
            h = [
                [
                    hbuf[t, pl.ds(to * 64 + q * 32 + k * 8, 8), par * 128 : par * 128 + 128]
                    for par in range(2)
                    for k in range(4)
                ]
                for q in range(2)
            ]
            for z, g_ref in enumerate((gbuf, gswap)):
                parts = []
                for p in range(4):
                    g = [g_ref[t * 64 + k * 8 : t * 64 + k * 8 + 8, p * 128 : p * 128 + 128] for k in range(8)]
                    for q in range(2):
                        terms = [a * b for a, b in zip(g, h[q])]
                        parts.append(functools.reduce(jnp.add, terms))
                v = rows_of_sums(parts)
                v = jnp.where(lane < 64, v, -v) if z == 0 else v
                v = jnp.where(lane == zl * 2 + t, jnp.sum(v, axis=1, keepdims=True), 0.0)
                totals[z] = v if totals[z] is None else totals[z] + v
        for z in range(2):
            msg[to, z * 8 : z * 8 + 8] = totals[z]

    def answer(d):
        return remote(msg.at[rot(zl, d)], res.at[zl], m_out, m_in, dev(zl_=rot(zl, d)))

    for d in (1, 2, 3):
        answer(d).start()
    res[zl] = msg[zl]
    drain(res.at[pl.ds(0, 3)], m_in)
    out[...] = jnp.sum(res[...], axis=0)[:, :8]

    drain(vbuf.at[pl.ds(0, 13), pl.ds(0, 56)], v_out)
    drain(vbuf.at[pl.ds(0, 15), pl.ds(0, 8)], r_out)

    @pl.when(middle)
    def _():
        drain(vbuf.at[pl.ds(0, 4), pl.ds(0, 56)], v_out)

    drain(abuf.at[0], a_rout)
    drain(cbuf.at[pl.ds(0, 3)], c_out)
    drain(piece8.at[pl.ds(0, 7)], p8_out)
    drain(piece4.at[pl.ds(0, 3)], p4_out)
    drain(slabs.at[pl.ds(0, 248)], s_out)
    drain(res.at[pl.ds(0, 3)], m_out)


def local(amplitudes, vectors, row_map, col_map):
    dma = pltpu.SemaphoreType.DMA
    got = pl.pallas_call(
        kernel,
        out_shape=pltpu.VMEM((16, 8), F32),
        in_specs=[pl.BlockSpec(memory_space=pl.ANY)] * 4,
        out_specs=pl.BlockSpec(memory_space=pltpu.VMEM),
        scratch_shapes=[
            pltpu.VMEM((2, 16, 64, 512), F32),
            pltpu.VMEM((16, 64, 512), F32),
            pltpu.VMEM((32, 4, 128), F32),
            pltpu.VMEM((4, 32, 2, 128), F32),
            pltpu.VMEM((256, 128), F32),
            pltpu.VMEM((64, 128), F32),
            pltpu.VMEM((8, 8, 128), F32),
            pltpu.VMEM((4, 8, 128), F32),
            pltpu.VMEM((256, 128), F32),
            pltpu.VMEM((4, 128, 128), F32),
            pltpu.VMEM((384, 512), BF16),
            pltpu.VMEM((256, 384), BF16),
            pltpu.VMEM((2, 384, 256), BF16),
            pltpu.VMEM((128, 512), F32),
            pltpu.VMEM((128, 512), F32),
            pltpu.VMEM((2, 256, 256), F32),
            pltpu.VMEM((4, 16, 128), F32),
            pltpu.VMEM((4, 16, 128), F32),
            dma, dma, dma, dma, dma((4, 2)), dma((4,)), dma((3,)), dma((4, 7)), dma, dma, dma((2,)), dma, dma,
            dma, dma, dma, dma, dma, dma, dma, dma, pltpu.SemaphoreType.REGULAR((3,)),
        ],
        compiler_params=pltpu.CompilerParams(collective_id=0, has_side_effects=True),
    )(
        amplitudes.reshape(64, -1),
        vectors,
        row_map.reshape(4, 32, 128).transpose(1, 0, 2),
        col_map.reshape(2, 32, 128).transpose(1, 0, 2),
    )
    return got.reshape(2, 4, 2, 8).transpose(0, 3, 1, 2)


def solution(mesh):
    return jax.shard_map(
        local,
        mesh=mesh,
        in_specs=(
            P(None, "bond", "leg"),
            P(None, ("leg", "bond")),
            P("leg", None),
            P("bond", None),
        ),
        out_specs=P(None, None, "leg", "bond"),
        check_vma=False,
    )
```

```python
import functools

import jax
import jax.numpy as jnp
from jax import lax
from jax.experimental import pallas as pl
from jax.experimental.pallas import tpu as pltpu
from jax.sharding import PartitionSpec as P

MESH = pl.DeviceIdType.MESH
F32, BF16 = jnp.float32, jnp.bfloat16
NT = (((1,), (1,)), ((), ()))
NN = (((1,), (0,)), ((), ()))


def halves(v):
    hi = v.astype(BF16)
    return hi, (v - hi.astype(F32)).astype(BF16)


def kernel(
    amp, vec, rmap, cmap, out,
    abuf, vbuf, rbuf, cbuf, acc, part, piece8, piece4, slabs, rwide, rcat, ccat, bcat, gbuf, gswap, hbuf, msg, res,
    a_in, a_rin, v_in, z_in, b_in, r_in, x_in, v_out, map_in, c_in, c_out, p8_in, p4_in, s_in, m_in, word,
):
    bond, leg = lax.axis_index("bond"), lax.axis_index("leg")
    core, x, zl = lax.rem(bond, 2), lax.rem(bond // 2, 4), bond // 8
    y, zh = lax.rem(leg, 4), leg // 4

    def dev(x_=x, zl_=zl, core_=core, y_=y, zh_=zh):
        return ((zl_ * 4 + x_) * 2 + core_, zh_ * 4 + y_)

    def rot(v, d):
        return lax.rem(v + (d + 4), 4)

    def remote(src, dst, send, recv, device):
        return pltpu.make_async_remote_copy(
            src_ref=src, dst_ref=dst, send_sem=send, recv_sem=recv, device_id=device, device_id_type=MESH
        )

    def drain(ref, sem):
        pltpu.make_async_copy(ref, ref, sem).wait()

    def up(d):
        z_ = lax.rem(zh * 4 + zl + (d + 16), 16)
        return dev(zl_=lax.rem(z_, 4), zh_=z_ // 4)

    middle = jnp.logical_and(zl > 0, zl < 3)
    edge = jnp.logical_not(middle)
    first = jnp.logical_or(jnp.logical_and(zl == 3, zh < 3), jnp.logical_and(zl == 0, zh == 0))
    inward = jnp.where(zl == 3, -1, 1)
    outside = up(-inward)
    inside = up(inward)
    beside = [dev(x_=rot(x, d)) for d in (1, -1)] + [dev(y_=rot(y, d)) for d in (1, -1)]
    partner = dev(core_=1 - core)
    rounds = (beside, [partner, up(2), up(-2)], [dev(y_=rot(y, d)) for d in (1, 2, 3)] + [up(4), up(-4)])

    def tell(sem, devices):
        for device in devices:
            pl.semaphore_signal(sem, inc=1, device_id=device, device_id_type=MESH)

    barrier = pltpu.get_barrier_semaphore()
    tell(barrier, beside[:2] + [inside] + beside[2:] + [partner])

    @pl.when(jnp.logical_or(middle, first))
    def _():
        tell(barrier, [outside])

    own = zl * 4 + x
    pltpu.make_async_copy(vec, vbuf.at[own], v_in).start()
    map_copies = (pltpu.make_async_copy(rmap, rbuf, map_in.at[0]), pltpu.make_async_copy(cmap, cbuf.at[zl], map_in.at[1]))
    for copy in map_copies:
        copy.start()

    def row_of(i):
        low, odd = zl < 2, lax.rem(zl, 2) == 1
        first = jnp.where(odd, 2, 1)
        second = jnp.where(odd, jnp.where(low, 0, 1), jnp.where(low, 2, 3))
        third = jnp.where(low, 3, 0)
        return jnp.where(i == 0, zl, jnp.where(i == 1, first, jnp.where(i == 2, second, third)))

    def block_of(i, xo):
        return row_of(i) * 4 + rot(x, xo)

    def a_local(n):
        cols = pl.ds(pl.multiple_of((n * 2 + core) * 512, 512), 512)
        return pltpu.make_async_copy(amp.at[:, cols], abuf.at[core, n], a_in)

    def a_remote(n):
        cols = pl.ds(pl.multiple_of((n * 2 + 1 - core) * 512, 512), 512)
        return remote(amp.at[:, cols], abuf.at[core, n], v_out, a_rin, dev(core_=1 - core))

    @pl.when(first)
    def _():
        pl.semaphore_wait(barrier, 6)

    @pl.when(jnp.logical_not(first))
    def _():
        pl.semaphore_wait(barrier, 7)


    rest = pl.ds(56, 8)

    def rows(half):
        return (pl.ds(0, 32), pl.ds(32, 24))[half]

    def side(k):
        return pl.ds(k * 256, 256)

    kinds = ((0, 1), (1, -1), (1, 1), (0, -1))

    def x_sem(i, half, k):
        return x_in.at[i, half * 2 + k if k < 2 else 4]

    def x_send(i, half, k):
        ref = vbuf.at[block_of(i, 0), rows(half), side(kinds[k][0])]
        return remote(ref, ref, v_out, x_sem(i, half, k), dev(x_=rot(x, kinds[k][1])))

    def x_relay(i, half, k):
        ref = vbuf.at[block_of(i, -kinds[k][1]), rows(half), side(kinds[k][0])]
        return remote(ref, ref, v_out, x_in.at[i, 5], dev(x_=rot(x, kinds[k][1])))

    def r_send(k):
        return remote(vec.at[rest], vbuf.at[own, rest], v_out, r_in.at[k], dev(x_=rot(x, kinds[k][1])))

    def r_relay(k):
        ref = vbuf.at[zl * 4 + rot(x, -kinds[k][1]), rest, side(k)]
        return remote(ref, ref, v_out, r_in.at[2], dev(x_=rot(x, kinds[k][1])))

    def b_send(i):
        ref = vbuf.at[pl.ds(zl * 4, 4), rest]
        return remote(ref, ref, v_out, b_in.at[zl], dev(zl_=row_of(i)))

    def b_take(i):
        ref = vbuf.at[pl.ds(row_of(i) * 4, 4), rest]
        remote(ref, ref, v_out, b_in.at[row_of(i)], dev()).wait_recv()

    def z_send(i, half):
        return remote(vec.at[rows(half)], vbuf.at[own, rows(half)], v_out, z_in.at[zl, half], dev(zl_=row_of(i)))

    def z_take(i, half):
        r = row_of(i)
        ref = vbuf.at[r * 4 + x, rows(half)]
        copy = remote(ref, ref, v_out, z_in.at[r, half], dev(zl_=jnp.where(r > zl, zl - 1, zl + 1)))
        copy.wait_recv()

        @pl.when(middle)
        def _():
            copy.start()

        for k in range(4):
            x_send(i, half, k).start()

    for k in (0, 1):
        r_send(k).start()
    for half in (0, 1):
        z_send(1, half).start()

        @pl.when(middle)
        def _():
            z_send(2, half).start()

        for k, (sd, way) in enumerate(kinds):
            at = (rows(half), side(sd))
            remote(vec.at[at], vbuf.at[(own, *at)], v_out, x_sem(0, half, k), dev(x_=rot(x, way))).start()
    def setup():
        tell(word.at[0], rounds[0])

        @pl.when(jnp.logical_not(first))
        def _():
            tell(word.at[0], [inside, outside])

        @pl.loop(0, 16)
        def _(m):
            n = block_of(m // 4, lax.rem(m, 4))
            a_local(n).start()
            a_remote(n).start()

    setup()
    pl.semaphore_wait(word.at[0], 6)

    @pl.when(first)
    def _():
        tell(word.at[0], [inside, outside])

    tell(word.at[1], rounds[1])
    acc[...] = jnp.zeros_like(acc)

    def project(n):
        a_hi, a_lo = halves(abuf[:, n].reshape(128, 512))
        v_hi, v_lo = halves(vbuf[n])
        acc[...] += lax.dot_general(
            jnp.concatenate([a_hi, a_lo], 0), jnp.concatenate([v_hi, v_lo], 0), NT, preferred_element_type=F32
        )

    def relay(i):
        for half in (0, 1):
            for k in (0, 1):
                x_send(i, half, k).wait_recv()
                x_relay(i, half, k).start()

    def near(i):
        project(block_of(i, 0))
        drain(vbuf.at[block_of(i, -1), pl.ds(0, 56)], x_in.at[i, 4])
        project(block_of(i, -1))
        project(block_of(i, 1))

    def far(i):
        n = block_of(i, 2)
        drain(vbuf.at[n, pl.ds(0, 56)], x_in.at[i, 5])
        project(n)

    for k in (0, 1):
        r_send(k).wait_recv()
        r_relay(k).start()
    c_sends = [
        remote(cbuf.at[zl], cbuf.at[zl], c_out, c_in, dev(zl_=rot(zl, d))) for d in (1, 2, 3)
    ]

    def maps():
        first = lax.broadcasted_iota(jnp.int32, (32, 128), 1) < 64
        for p in range(4):
            v = rbuf[:, p, :]
            swapped = pltpu.roll(v, 64, 1)
            for par in range(2):
                low, high = (v, swapped) if par == 0 else (swapped, v)
                rwide[p, pl.ds(par, 32, stride=2)] = jnp.where(first, low, 0.0)
                rwide[p, pl.ds(64 + par, 32, stride=2)] = jnp.where(first, 0.0, high)
            hi, lo = halves(rwide[p])
            for k, w in enumerate((hi, hi, lo)):
                rcat[k * 128 : k * 128 + 128, p * 128 : p * 128 + 128] = w
        bcat[...] = jnp.zeros_like(bcat)
        drain(cbuf.at[pl.ds(0, 3)], c_in)
        for k in range(4):
            for q in range(2):
                hi, lo = halves(cbuf[k, :, q, :])
                ccat[k * 64 + q * 32 : k * 64 + q * 32 + 32] = jnp.concatenate([hi, lo, hi], 1)

    pltpu.make_async_copy(vec, vbuf.at[own], v_in).wait()

    next_row = jnp.where(middle, 3, 2)

    z_take(1, 0)
    z_take(1, 1)

    @pl.when(middle)
    def _():
        z_take(2, 0)
        z_take(2, 1)

    relay(0)
    z_take(next_row, 0)
    drain(vbuf.at[own, rest], r_in.at[2])
    z_take(next_row, 1)
    pl.semaphore_wait(word.at[1], 3)
    tell(word.at[2], rounds[2])

    def bundles():
        for i in (1, 2, 3):
            b_send(i).start()

    pl.when(core == 0)(bundles)
    relay(1)
    drain(abuf.at[core], a_in)
    drain(abuf.at[1 - core], a_rin)

    @pl.when(middle)
    def _():
        near(0)
        far(0)

    @pl.when(edge)
    def _():
        z_take(3, 0)
        z_take(3, 1)

    relay(2)
    pl.when(core == 1)(bundles)

    @pl.when(middle)
    def _():
        relay(3)

    @pl.when(edge)
    def _():
        near(0)
        far(0)

    b_take(1)
    near(1)

    @pl.when(edge)
    def _():
        relay(3)

    for copy in map_copies:
        copy.wait()
    for copy in c_sends:
        copy.start()
    b_take(2)
    near(2)
    far(1)
    b_take(3)
    near(3)
    far(2)
    far(3)

    both = acc[:128] + acc[128:]
    both = both + pltpu.roll(both, 64, 1)
    first = lax.broadcasted_iota(jnp.int32, (32, 128), 1) < 64
    for s in range(2):
        part[s * 32 : s * 32 + 32] = jnp.where(first, both[s * 64 : s * 64 + 32], both[s * 64 + 32 : s * 64 + 64])

    pl.semaphore_wait(word.at[2], 5)
    mine = y * 2 + core

    def eighth(k):
        return pl.ds(pl.multiple_of(k * 8, 8), 8)

    def scatter(k):
        to = lax.rem(mine + k, 8)
        return remote(part.at[eighth(to)], piece8.at[mine], v_out, p8_in, dev(y_=to // 2, core_=lax.rem(to, 2)))

    for k in (5, 4, 3, 2, 6, 7, 1):
        scatter(k).start()
    piece8[mine] = part[eighth(mine)]
    drain(piece8.at[pl.ds(0, 7)], p8_in)
    piece4[zh] = jnp.sum(piece8[...], axis=0)

    def spread(d):
        return remote(piece4.at[zh], piece4.at[zh], v_out, p4_in, dev(zh_=rot(zh, d)))

    for d in (2, 1, 3):
        spread(d).start()
    maps()
    drain(piece4.at[pl.ds(0, 3)], p4_in)
    here = pl.ds(pl.multiple_of(x * 64 + mine * 8, 8), 8)
    slabs[here] = jnp.sum(piece4[...], axis=0)

    for dx in (2, 1, 3, 0):
        for dy in (2, 1, 3, 0):
            for core_ in (1 - core, core):
                if dx or dy or core_ is not core:
                    to = dev(x_=rot(x, dx), y_=rot(y, dy), core_=core_)
                    remote(slabs.at[here], slabs.at[here], v_out, s_in, to).start()

    drain(slabs.at[pl.ds(0, 248)], s_in)

    lhs = jnp.concatenate(
        [slabs[pl.ds(t * 128 + par, 32, stride=2)] for t in range(2) for par in range(2)], 0
    )
    l_hi, l_lo = halves(lhs)
    gbuf[...] = lax.dot_general(
        jnp.concatenate([l_hi, l_lo, l_hi], 1), rcat[...], NN, preferred_element_type=F32
    )
    for p in range(4):
        cols = slice(p * 128, p * 128 + 128)
        gswap[:, cols] = pltpu.roll(gbuf[:, cols], 64, 1)
    for t in range(2):
        b_hi, b_lo = halves(slabs[t * 128 + 64 : t * 128 + 128])
        for k, v in enumerate((b_hi, b_hi, b_lo)):
            for par in range(2):
                bcat[t, k * 128 + par * 64 : k * 128 + par * 64 + 64, par * 128 : par * 128 + 128] = v
        hbuf[t] = lax.dot_general(ccat[...], bcat[t], NN, preferred_element_type=F32)

    row = lax.broadcasted_iota(jnp.int32, (8, 128), 0)
    lane = lax.broadcasted_iota(jnp.int32, (8, 128), 1)

    def rows_of_sums(parts):
        for shift in (1, 2, 4):
            even = row % (2 * shift) < shift
            parts = [
                jnp.where(even, a, b) + pltpu.roll(jnp.where(even, b, a), shift, 0)
                for a, b in zip(parts[::2], parts[1::2])
            ]
        return parts[0]

    for to in range(4):
        totals = [None, None]
        for t in range(2):
            h = [
                [
                    hbuf[t, pl.ds(to * 64 + q * 32 + k * 8, 8), par * 128 : par * 128 + 128]
                    for par in range(2)
                    for k in range(4)
                ]
                for q in range(2)
            ]
            for z, g_ref in enumerate((gbuf, gswap)):
                parts = []
                for p in range(4):
                    g = [g_ref[t * 64 + k * 8 : t * 64 + k * 8 + 8, p * 128 : p * 128 + 128] for k in range(8)]
                    for q in range(2):
                        terms = [a * b for a, b in zip(g, h[q])]
                        parts.append(functools.reduce(jnp.add, terms))
                v = rows_of_sums(parts)
                v = jnp.where(lane < 64, v, -v) if z == 0 else v
                v = jnp.where(lane == zl * 2 + t, jnp.sum(v, axis=1, keepdims=True), 0.0)
                totals[z] = v if totals[z] is None else totals[z] + v
        for z in range(2):
            msg[to, z * 8 : z * 8 + 8] = totals[z]

    def answer(d):
        return remote(msg.at[rot(zl, d)], res.at[zl], v_out, m_in, dev(zl_=rot(zl, d)))

    for d in (1, 2, 3):
        answer(d).start()
    res[zl] = msg[zl]
    drain(res.at[pl.ds(0, 3)], m_in)
    out[...] = jnp.sum(res[...], axis=0)[:, :8]

    drain(vbuf.at[pl.ds(0, 13), pl.ds(0, 56)], v_out)
    drain(vbuf.at[pl.ds(0, 15), pl.ds(0, 8)], v_out)

    @pl.when(middle)
    def _():
        drain(vbuf.at[pl.ds(0, 4), pl.ds(0, 56)], v_out)

    drain(abuf.at[0], v_out)
    drain(cbuf.at[pl.ds(0, 3)], c_out)
    drain(piece8.at[pl.ds(0, 7)], v_out)
    drain(piece4.at[pl.ds(0, 3)], v_out)
    drain(slabs.at[pl.ds(0, 248)], v_out)
    drain(res.at[pl.ds(0, 3)], v_out)


def local(amplitudes, vectors, row_map, col_map):
    dma = pltpu.SemaphoreType.DMA
    got = pl.pallas_call(
        kernel,
        out_shape=pltpu.VMEM((16, 8), F32),
        in_specs=[pl.BlockSpec(memory_space=pl.ANY)] * 4,
        out_specs=pl.BlockSpec(memory_space=pltpu.VMEM),
        scratch_shapes=[
            pltpu.VMEM((2, 16, 64, 512), F32),
            pltpu.VMEM((16, 64, 512), F32),
            pltpu.VMEM((32, 4, 128), F32),
            pltpu.VMEM((4, 32, 2, 128), F32),
            pltpu.VMEM((256, 128), F32),
            pltpu.VMEM((64, 128), F32),
            pltpu.VMEM((8, 8, 128), F32),
            pltpu.VMEM((4, 8, 128), F32),
            pltpu.VMEM((256, 128), F32),
            pltpu.VMEM((4, 128, 128), F32),
            pltpu.VMEM((384, 512), BF16),
            pltpu.VMEM((256, 384), BF16),
            pltpu.VMEM((2, 384, 256), BF16),
            pltpu.VMEM((128, 512), F32),
            pltpu.VMEM((128, 512), F32),
            pltpu.VMEM((2, 256, 256), F32),
            pltpu.VMEM((4, 16, 128), F32),
            pltpu.VMEM((4, 16, 128), F32),
            dma, dma, dma, dma((4, 2)), dma((4,)), dma((3,)), dma((4, 6)), dma, dma((2,)), dma, dma,
            dma, dma, dma, dma, pltpu.SemaphoreType.REGULAR((3,)),
        ],
        compiler_params=pltpu.CompilerParams(collective_id=0, has_side_effects=True),
    )(
        amplitudes.reshape(64, -1),
        vectors,
        row_map.reshape(4, 32, 128).transpose(1, 0, 2),
        col_map.reshape(2, 32, 128).transpose(1, 0, 2),
    )
    return got.reshape(2, 4, 2, 8).transpose(0, 3, 1, 2)


def solution(mesh):
    return jax.shard_map(
        local,
        mesh=mesh,
        in_specs=(
            P(None, "bond", "leg"),
            P(None, ("leg", "bond")),
            P("leg", None),
            P("bond", None),
        ),
        out_specs=P(None, None, "leg", "bond"),
        check_vma=False,
    )
```
